128 devices in a mesh: brick: 8 (over z, core), view: 16 (over y, x).
Axes of the slice: x: 4, y: 4, z: 4, core: 2. Of those that a mesh axis runs over, the one named last changes fastest.
Arguments:
- latent_grid: bfloat16 [8, 16, 32768], P('brick'), may hold values from -6 to 6
- layer_one: bfloat16 [64, 16], replicated, may hold values from -1.5 to 1.5
- layer_two: bfloat16 [64, 64], replicated, may hold values from -0.75 to 0.75
- layer_three: bfloat16 [64, 64], replicated, may hold values from -0.75 to 0.75
- layer_four: bfloat16 [33, 64], replicated, may hold values from -0.75 to 0.75
- view_order: int32 [16], P('view'), may hold values from 0 to 7
- samples: int32 [16, 8, 8, 4096], P('view', 'brick'), may hold values from 0 to 32767, as said below
- pixel_grad: float32 [16, 32, 4096], P('view', None, 'brick'), may hold values from -24 to 24
Outputs:
- composite: float32 [16, 32, 4096], P('view', None, 'brick')
- latent_grad: float32 [8, 16, 32768], P('brick')
- layer_one_grad: float32 [64, 16], replicated
- layer_two_grad: float32 [64, 64], replicated
- layer_three_grad: float32 [64, 64], replicated
- layer_four_grad: float32 [33, 64], replicated
The draws below stay inside these ranges and needn't reach their ends.
Inputs may be any that keep to these rules, and one draw needn't show every extreme that they name: The depth rank of brick b in view v is b xor view_order[v]. `samples`: sample step s of pixel p reads a voxel from s * 4096 + (p // 512) * 512 to that plus 512 - 1.
All inputs are finite; a program needn't handle non-finite values.
Results may differ from the reference program's by a relative error of at most 0.015.
Values sent between devices are 32-bit elements; how exact they have to be, the bound alone decides.
No kernel may reach another device: no remote copies, remote signals or barrier semaphores. Data moves between devices by JAX's collectives and lax.ppermute only.
A program may use at most 128 MiB of HBM per device.

```python
import jax
import jax.numpy as jnp
from jax import lax

C_LAT = 16
HIDDEN_SIZE = 64
COLOURS = 32
RAY_STEPS = 8
PIX_DEV = 4096
VOXELS = 32768
SLAB = 4096
TILE_VOX = 512
TILE_PIX = 512
VIEWS = 16
BRICKS = 8
N_BRICK = 8


def draw_samples(key, part):
    shape = (VIEWS, BRICKS, RAY_STEPS, PIX_DEV)
    local = jax.random.randint(key, shape, 0, TILE_VOX).astype(jnp.int32)
    local = local.at[:, :, 0, 0].set(0)
    local = local.at[:, :, RAY_STEPS - 1, PIX_DEV - 1].set(TILE_VOX - 1)
    step_base = lax.broadcasted_iota(jnp.int32, shape, 2) * SLAB
    tile_base = lax.broadcasted_iota(jnp.int32, shape, 3) // TILE_PIX * TILE_VOX
    return (local + step_base + tile_base).astype(jnp.int32)


def place_ends(drawn, stream_key, smallest, high):
    longest = drawn.shape.index(max(drawn.shape))
    spots = []
    for shift in (0, 1):
        where = [jax.random.randint(jax.random.fold_in(stream_key, axis), (), 0, length) for axis, length in enumerate(drawn.shape)]
        where[longest] = (where[longest] + shift) % drawn.shape[longest]
        spots.append(tuple(where))
    return drawn.at[spots[0]].set(smallest).at[spots[1]].set(high)


def level_of(rng, dims, shards, low, high):
    loudness = 1.0
    for axis_at, blocks in shards:
        steps = jax.random.uniform(jax.random.fold_in(jax.random.fold_in(rng, 6), axis_at), (blocks,), jnp.float32, low / len(shards), high / len(shards))
        loudness = loudness * jnp.repeat(jnp.exp(steps), dims[axis_at] // blocks).reshape((-1,) + (1,) * (len(dims) - 1 - axis_at))
    return loudness


def gaussian(rng, shape, scale, limit, shards=(), kind=jnp.bfloat16):
    level = level_of(rng, shape, shards, -0.22, 0.18) if shards else 1.0
    values = jax.random.normal(rng, shape, jnp.float32) * scale * level
    return jnp.minimum(jnp.maximum(values, -limit), limit).astype(kind)


def setup_inputs(seed: int = 0) -> dict:
    streams_of = jax.random.split(jax.random.key(seed), 9)
    return {
        "latent_grid": gaussian(streams_of[0], (BRICKS, C_LAT, VOXELS), 1.0, 6.0, ((0, 8),)),
        "layer_one": gaussian(streams_of[1], (HIDDEN_SIZE, C_LAT), C_LAT ** -0.5, 1.5),
        "layer_two": gaussian(streams_of[2], (HIDDEN_SIZE, HIDDEN_SIZE), HIDDEN_SIZE ** -0.5, 0.75),
        "layer_three": gaussian(streams_of[3], (HIDDEN_SIZE, HIDDEN_SIZE), HIDDEN_SIZE ** -0.5, 0.75),
        "layer_four": gaussian(streams_of[4], (COLOURS + 1, HIDDEN_SIZE), HIDDEN_SIZE ** -0.5, 0.75),
        "view_order": place_ends(jax.random.randint(streams_of[5], (VIEWS,), 0, N_BRICK), jax.random.fold_in(streams_of[5], 1), 0, N_BRICK - 1).astype(jnp.int32),
        "samples": draw_samples(jax.random.fold_in(streams_of[8], 71), 0),
        "pixel_grad": gaussian(streams_of[7], (VIEWS, COLOURS, PIX_DEV), 4.0, 24.0, ((0, 16), (2, 8)), jnp.float32),
    }


def brick_forward(features, first, second, third, fourth, spacing, ray_count):
    inputs = features.astype(jnp.bfloat16)
    hidden = jax.nn.silu(jnp.dot(first.astype(jnp.bfloat16), inputs, preferred_element_type=jnp.float32)).astype(jnp.bfloat16)
    hidden = jax.nn.silu(jnp.dot(second.astype(jnp.bfloat16), hidden, preferred_element_type=jnp.float32)).astype(jnp.bfloat16)
    hidden = jax.nn.silu(jnp.dot(third.astype(jnp.bfloat16), hidden, preferred_element_type=jnp.float32)).astype(jnp.bfloat16)
    output = jnp.dot(fourth.astype(jnp.bfloat16), hidden, preferred_element_type=jnp.float32)
    output = output.reshape(output.shape[0], ray_count, output.shape[1] // ray_count)
    colour = jax.nn.sigmoid(output[:-1])
    depth = jax.nn.softplus(output[-1]) * spacing
    running = jnp.cumsum(depth, axis=0)
    earlier = jnp.concatenate([jnp.zeros_like(depth[:1]), running[:-1]], axis=0)
    factor = jnp.exp(-earlier) * -jnp.expm1(-depth)
    partial_image = lax.optimization_barrier(jnp.sum(factor[None] * colour, axis=1))
    return (partial_image, jnp.exp(-running[-1]))

def reference(latent_grid, layer_one, layer_two, layer_three, layer_four, view_order, samples, pixel_grad):
    weights = (layer_one.astype(jnp.float32), layer_two.astype(jnp.float32), layer_three.astype(jnp.float32), layer_four.astype(jnp.float32))
    spacing = 2.0 / (RAY_STEPS * N_BRICK)
    bricks = latent_grid.shape[0]
    voxels = latent_grid.shape[2]

    def forward_local(features, first, second, third, fourth):
        return brick_forward(features, first, second, third, fourth, spacing, RAY_STEPS)

    def per_view(carry, inputs):
        order_value, view_samples, view_grad = inputs

        def features_of(brick_id):
            return latent_grid[brick_id][:, view_samples[brick_id].reshape(-1)].astype(jnp.float32)

        def forward_one(brick_id):
            return forward_local(features_of(brick_id), *weights)
        partials, transes = lax.map(forward_one, jnp.arange(bricks, dtype=jnp.int32))
        order = jnp.bitwise_xor(jnp.arange(bricks, dtype=jnp.int32), order_value)
        ordered_c = partials[order]
        ordered_t = transes[order]
        front = [jnp.ones_like(ordered_t[0])]
        for rank_id in range(bricks - 1):
            front.append(front[-1] * ordered_t[rank_id])
        behind = [jnp.zeros_like(ordered_c[0])]
        for rank_id in range(bricks - 1, 0, -1):
            behind.append(ordered_c[rank_id] + ordered_t[rank_id][None] * behind[-1])
        behind = behind[::-1]
        image = front[0][None] * ordered_c[0]
        for rank_id in range(1, bricks):
            image = image + front[rank_id][None] * ordered_c[rank_id]
        grad_c = jnp.stack([front[r][None] * view_grad for r in range(bricks)])
        grad_t = jnp.stack([front[r] * lax.optimization_barrier(jnp.sum(view_grad * behind[r], axis=0)) for r in range(bricks)])
        grad_c = grad_c[order]
        grad_t = grad_t[order]

        def backward_one(brick_id):
            index = view_samples[brick_id].reshape(-1)
            unused, pull = jax.vjp(forward_local, features_of(brick_id), *weights)
            pulled = pull((grad_c[brick_id], grad_t[brick_id]))
            grid_part = jnp.zeros((latent_grid.shape[1], voxels), jnp.float32).at[:, index].add(pulled[0])
            return (grid_part, pulled[1], pulled[2], pulled[3], pulled[4])
        grid_parts, g_one, g_two, g_three, g_four = lax.map(backward_one, jnp.arange(bricks, dtype=jnp.int32))
        carry = (carry[0] + grid_parts, carry[1] + lax.optimization_barrier(jnp.sum(g_one, 0)), carry[2] + lax.optimization_barrier(jnp.sum(g_two, 0)), carry[3] + lax.optimization_barrier(jnp.sum(g_three, 0)), carry[4] + lax.optimization_barrier(jnp.sum(g_four, 0)))
        return (carry, image)
    start = (jnp.zeros(latent_grid.shape, jnp.float32), jnp.zeros(layer_one.shape, jnp.float32), jnp.zeros(layer_two.shape, jnp.float32), jnp.zeros(layer_three.shape, jnp.float32), jnp.zeros(layer_four.shape, jnp.float32))
    totals, images = lax.scan(per_view, start, (view_order, samples, pixel_grad))
    return (images, totals[0], totals[1], totals[2], totals[3], totals[4])
```

```python
import functools

import jax
import jax.numpy as jnp
from jax import lax
from jax.experimental import pallas as pl
from jax.experimental.pallas import tpu as pltpu
from jax.sharding import PartitionSpec as P


F32 = jnp.float32
BF16 = jnp.bfloat16
NT = (((1,), (1,)), ((), ()))
STEPS = 8
TILE = 512
LANES = 128
PARTS = TILE // LANES
OUT_ROWS = 40


def mm(a, b):
    return jnp.dot(a, b, preferred_element_type=F32)


def mm_nt(a, b):
    return lax.dot_general(a, b, NT, preferred_element_type=F32)


def place_to_tile(place, brick):
    return jnp.bitwise_xor(jnp.bitwise_xor(place, jnp.right_shift(place, 2) * 2), brick)


def one_hot(local):
    low = jnp.bitwise_and(local, LANES - 1)
    rows = lax.broadcasted_iota(jnp.int32, (LANES, local.shape[1]), 0)
    return jnp.where(rows == low, 1.0, 0.0).astype(BF16)


def row_of(array, step):
    return array[step : step + 1, :]


def forward_kernel(
    brick_ref, grid_ref, samples_ref, one_ref, two_ref, three_ref, four_ref,
    partial_ref, trans_ref, hidden_ref, feature_ref, colour_ref, ray_ref, last_ref,
):
    place = pl.program_id(0)
    tile = place_to_tile(place, brick_ref[0])
    spacing = 2.0 / (STEPS * 8)
    channels = grid_ref.shape[0]
    for step in range(STEPS):
        span = pl.ds(step * TILE, TILE)
        local = jnp.bitwise_and(samples_ref[step : step + 1, :], TILE - 1)
        base = step * (grid_ref.shape[1] // STEPS) + tile * TILE
        pieces = [
            grid_ref[:, pl.ds(pl.multiple_of(base + k * LANES, LANES), LANES)]
            for k in range(PARTS)
        ]
        wide = mm(jnp.concatenate(pieces, axis=0), one_hot(local))
        high = jnp.broadcast_to(jnp.right_shift(local, 7), (channels, TILE))
        picked = wide[:channels]
        for k in range(1, PARTS):
            picked = jnp.where(high == k, wide[k * channels : (k + 1) * channels], picked)
        value = picked.astype(BF16)
        feature_ref[0, :, span] = value
        for layer, weight_ref in enumerate((one_ref, two_ref, three_ref)):
            half = mm(weight_ref[...], value)
            gate = 1.0 + jnp.tanh(half)
            hidden = half * gate
            value = hidden.astype(BF16)
            hidden_ref[0, layer, :, span] = value
            hidden_ref[0, 3 + layer, :, span] = (gate + hidden * (2.0 - gate)).astype(BF16)
        output = mm(four_ref[...], value)
        colour_ref[0, :, span] = 0.5 + 0.5 * jnp.tanh(output[:32])
        last_ref[step : step + 1, :] = output[32:33]
    half = last_ref[...]
    raw = half + half
    depth = (jnp.maximum(raw, 0.0) + jnp.log1p(jnp.exp(-jnp.abs(raw)))) * spacing
    running = [row_of(depth, 0)]
    for step in range(1, STEPS):
        running.append(running[-1] + row_of(depth, step))
    earlier = jnp.concatenate([jnp.zeros_like(running[0])] + running[:-1], axis=0)
    running = jnp.concatenate(running, axis=0)
    through = jnp.exp(-running)
    small = depth * (1.0 - depth * (0.5 - depth * (1.0 / 6.0 - depth * (1.0 / 24.0))))
    absorbed = jnp.where(depth < 0.02, small, 1.0 - jnp.exp(-depth))
    factor = jnp.exp(-earlier) * absorbed
    ray_ref[0, 0] = factor
    ray_ref[0, 1] = through
    ray_ref[0, 2] = spacing * (0.5 + 0.5 * jnp.tanh(half))
    image = row_of(factor, 0) * colour_ref[0, :, 0:TILE]
    for step in range(1, STEPS):
        image = image + row_of(factor, step) * colour_ref[0, :, step * TILE : (step + 1) * TILE]
    partial_ref[0] = image
    trans_ref[pl.ds(place, 1), :] = through[STEPS - 1 : STEPS, :]


def backward_kernel(
    brick_ref, samples_ref, given_ref, weight_ref, behind_ref, hidden_ref, feature_ref,
    colour_ref, ray_ref, one_ref, two_ref, three_ref, four_ref,
    grid_ref, packed_ref, cot_ref, out_ref,
):
    place = pl.program_id(0)
    channels = feature_ref.shape[1]
    weight = weight_ref[pl.ds(place, 1), :]
    trans_grad = weight * behind_ref[pl.ds(place, 1), :]
    factor = ray_ref[0, 0]
    through = ray_ref[0, 1]
    scaled = weight * given_ref[0]
    dots = jnp.concatenate(
        [
            jnp.sum(scaled * colour_ref[0, :, step * TILE : (step + 1) * TILE], axis=0, keepdims=True)
            for step in range(STEPS)
        ],
        axis=0,
    )
    taken = factor * dots
    later = [row_of(through, STEPS - 1) * trans_grad]
    for step in range(STEPS - 1, 0, -1):
        later.append(later[-1] + row_of(taken, step))
    depth_grad = through * dots - jnp.concatenate(later[::-1], axis=0)
    last = depth_grad * ray_ref[0, 2]
    first_row = lax.broadcasted_iota(jnp.int32, (OUT_ROWS - 32, TILE), 0) == 0
    for step in range(STEPS):
        span = pl.ds(step * TILE, TILE)
        colour = colour_ref[0, :, step * TILE : (step + 1) * TILE]
        out_cot = jnp.concatenate(
            [
                (colour - colour * colour) * (row_of(factor, step) * scaled),
                jnp.where(first_row, row_of(last, step), 0.0),
            ],
            axis=0,
        ).astype(BF16)
        out_ref[:, span] = out_cot
        cot = out_cot
        for layer, weight_t_ref in ((2, four_ref), (1, three_ref), (0, two_ref)):
            cot = mm(weight_t_ref[...], cot).astype(BF16) * hidden_ref[0, 3 + layer, :, span]
            cot_ref[layer, :, span] = cot
        feature_cot = mm(one_ref[...], cot).astype(BF16).astype(F32)
        local = jnp.bitwise_and(samples_ref[step : step + 1, :], TILE - 1)
        high = jnp.broadcast_to(jnp.right_shift(local, 7), (channels, TILE))
        spread = jnp.concatenate(
            [jnp.where(high == k, feature_cot, 0.0) for k in range(PARTS)], axis=0
        ).astype(BF16)
        grid_ref[0, step] = mm_nt(spread, one_hot(local))

    @pl.when(place == 0)
    def _():
        packed_ref[...] = jnp.zeros_like(packed_ref)

    packed_ref[0:64, 0:64] += 0.5 * mm_nt(cot_ref[1], hidden_ref[0, 0])
    packed_ref[0:64, 64:128] += 0.5 * mm_nt(cot_ref[2], hidden_ref[0, 1])
    packed_ref[64:104, 0:64] += mm_nt(out_ref[...], hidden_ref[0, 2])
    packed_ref[64:80, 64:128] += 0.5 * mm_nt(feature_ref[0], cot_ref[0])


def whole(shape):
    return pl.BlockSpec(shape, lambda p, brick: (0,) * len(shape))


def at_place(shape):
    return pl.BlockSpec((1,) + shape, lambda p, brick: (p,) + (0,) * len(shape))


def run_forward(brick, grid, samples, one, two, three, four):
    tiles = 8
    wide = STEPS * TILE
    channels = grid.shape[0]
    shapes = [
        jax.ShapeDtypeStruct((tiles, 32, TILE), F32),
        jax.ShapeDtypeStruct((tiles, TILE), F32),
        jax.ShapeDtypeStruct((tiles, 6, 64, wide), BF16),
        jax.ShapeDtypeStruct((tiles, channels, wide), BF16),
        jax.ShapeDtypeStruct((tiles, 32, wide), F32),
        jax.ShapeDtypeStruct((tiles, 3, STEPS, TILE), F32),
    ]
    return pl.pallas_call(
        forward_kernel,
        out_shape=shapes,
        grid_spec=pltpu.PrefetchScalarGridSpec(
            num_scalar_prefetch=1,
            grid=(tiles,),
            in_specs=[
                whole(grid.shape),
                pl.BlockSpec((STEPS, TILE), lambda p, brick: (0, place_to_tile(p, brick[0]))),
                whole(one.shape),
                whole(two.shape),
                whole(three.shape),
                whole(four.shape),
            ],
            out_specs=[
                at_place((32, TILE)),
                whole((tiles, TILE)),
                at_place((6, 64, wide)),
                at_place((channels, wide)),
                at_place((32, wide)),
                at_place((3, STEPS, TILE)),
            ],
            scratch_shapes=[pltpu.VMEM((STEPS, TILE), F32)],
        ),
        cost_estimate=pl.CostEstimate(
            flops=2_000_000_000, bytes_accessed=32_000_000, transcendentals=8_000_000
        ),
        name="forward",
    )(brick, grid, samples, one, two, three, four)


def run_backward(brick, samples, given, weight, behind, saved, one, two, three, four):
    tiles = 8
    wide = STEPS * TILE
    hidden, feature, colour, ray = saved
    channels = feature.shape[1]
    return pl.pallas_call(
        backward_kernel,
        out_shape=[
            jax.ShapeDtypeStruct((tiles, STEPS, PARTS * channels, LANES), F32),
            jax.ShapeDtypeStruct((128, 128), F32),
        ],
        grid_spec=pltpu.PrefetchScalarGridSpec(
            num_scalar_prefetch=1,
            grid=(tiles,),
            in_specs=[
                pl.BlockSpec((STEPS, TILE), lambda p, brick: (0, place_to_tile(p, brick[0]))),
                at_place((32, TILE)),
                whole((tiles, TILE)),
                whole((tiles, TILE)),
                at_place((6, 64, wide)),
                at_place((channels, wide)),
                at_place((32, wide)),
                at_place((3, STEPS, TILE)),
                whole(one.shape),
                whole(two.shape),
                whole(three.shape),
                whole(four.shape),
            ],
            out_specs=[
                pl.BlockSpec(
                    (1, STEPS, PARTS * channels, LANES),
                    lambda p, brick: (place_to_tile(p, brick[0]), 0, 0, 0),
                ),
                whole((128, 128)),
            ],
            scratch_shapes=[
                pltpu.VMEM((3, 64, wide), BF16),
                pltpu.VMEM((OUT_ROWS, wide), BF16),
            ],
        ),
        cost_estimate=pl.CostEstimate(
            flops=4_000_000_000, bytes_accessed=36_000_000, transcendentals=0
        ),
        name="backward",
    )(brick, samples, given, weight, behind, hidden, feature, colour, ray, one, two, three, four)


def swap_brick(array, flip):
    return lax.ppermute(array, "brick", [(i, i ^ flip) for i in range(8)])


def swap_rows(array, flip):
    parts = array.reshape((8 // (2 * flip), 2, flip) + array.shape[1:])
    return jnp.flip(parts, axis=1).reshape(array.shape)


def view_swap(array, dim):
    flip = 1 if dim < 2 else 3
    pairs = []
    for y in range(4):
        for x in range(4):
            other = (y, x ^ flip) if dim % 2 == 0 else (y ^ flip, x)
            pairs.append((y * 4 + x, other[0] * 4 + other[1]))
    return lax.ppermute(array, "view", pairs)


def view_bits():
    view = lax.axis_index("view")
    y = view // 4
    x = view % 4
    return [
        jnp.bitwise_and(x ^ (x >> 1), 1),
        jnp.bitwise_and(y ^ (y >> 1), 1),
        x >> 1,
        y >> 1,
    ]


def pick(array, index):
    return lax.dynamic_index_in_dim(array, index, 0, False)


def sum_over_views(grid, packed):
    bits = view_bits()
    parts = [grid[c] for c in range(4)]
    extra = packed
    for flip in (1, 2):
        extra = extra + swap_brick(extra, flip)
    extra = extra + swap_brick(extra, 6)
    extra = [extra[c * 32 : (c + 1) * 32] for c in range(4)]
    for turn in range(2):
        dims = [(c + turn) % 4 for c in range(4)]
        got = [view_swap(pick(parts[c], 1 - bits[dims[c]]), dims[c]) for c in range(4)]
        parts = [pick(parts[c], bits[dims[c]]) + got[c] for c in range(4)]
    inner = parts[0].shape
    rows = parts[0].size // 128
    for turn in range(2, 4):
        dims = [(c + turn) % 4 for c in range(4)]
        sent = [jnp.concatenate([parts[c].reshape(rows, 128), extra[c]], 0) for c in range(4)]
        got = [view_swap(sent[c], dims[c]) for c in range(4)]
        parts = [parts[c] + got[c][:rows].reshape(inner) for c in range(4)]
        extra = [extra[c] + got[c][rows:] for c in range(4)]
    for turn in (1, 0):
        dims = [(c + turn) % 4 for c in range(4)]
        rows = parts[0].size // 128
        shape = parts[0].shape
        sent = [jnp.concatenate([parts[c].reshape(rows, 128), extra[c]], 0) for c in range(4)]
        got = [view_swap(sent[c], dims[c]) for c in range(4)]
        extra = [extra[c] + got[c][rows:] for c in range(4)]
        got = [g[:rows].reshape(shape) for g in got]
        parts = [
            jnp.where(
                bits[dims[c]] == 0, jnp.stack([parts[c], got[c]]), jnp.stack([got[c], parts[c]])
            )
            for c in range(4)
        ]
    return jnp.stack(parts), jnp.concatenate(extra, axis=0)


def body(
    latent_grid, layer_one, layer_two, layer_three, layer_four, view_order, samples, pixel_grad
):
    brick_id = lax.axis_index("brick")
    rank = jnp.bitwise_xor(brick_id, view_order[0])
    brick = jnp.reshape(brick_id, (1,)).astype(jnp.int32)
    channels, voxels = latent_grid.shape[1:]
    index = samples[0, 0]
    half_one = layer_one * 0.5
    half_two = layer_two * 0.5
    half_three = layer_three * 0.5
    four = jnp.pad(layer_four, ((0, OUT_ROWS - 33), (0, 0)))

    given = pixel_grad
    for flip in (1, 2, 6):
        given = jnp.concatenate([given, swap_brick(given, flip)], axis=0)

    partial, trans, *saved = run_forward(
        brick, latent_grid[0], index, half_one, half_two, half_three, four * 0.5
    )

    dots = jnp.sum(partial * given, axis=1)
    total, front = trans, jnp.ones_like(trans)
    after, behind = jnp.ones_like(trans), jnp.zeros_like(trans)
    for level, (flip, rows) in enumerate(((1, 1), (2, 2), (6, 4))):
        got = swap_brick(jnp.stack([total, dots]), flip)
        got_total = swap_rows(got[0], rows)
        got_dots = swap_rows(got[1], rows)
        first = jnp.bitwise_and(jnp.right_shift(rank, level), 1) == 0
        behind = jnp.where(first, behind + after * got_dots, behind)
        after = jnp.where(first, after * got_total, after)
        front = jnp.where(first, front, front * got_total)
        dots = jnp.where(first, dots + total * got_dots, got_dots + got_total * dots)
        total = total * got_total

    image = front[:, None, :] * partial
    for flip, keep in ((6, 4), (2, 2), (1, 1)):
        image = image[:keep] + swap_brick(image[keep:], flip)

    grid, packed = run_backward(
        brick, index, given, front, behind, saved,
        half_one.T, half_two.T, half_three.T, four.T,
    )
    shape = grid.shape
    grid, packed = sum_over_views(grid.reshape((4, 2, 2, 4) + shape[2:]), packed)
    grid = grid.reshape(8, STEPS, PARTS, channels, LANES).transpose(3, 1, 0, 2, 4)
    return (
        image,
        grid.reshape(1, channels, voxels),
        packed[64:80, 64:128].T,
        packed[0:64, 0:64],
        packed[0:64, 64:128],
        packed[64:97, 0:64],
    )


def solution(mesh):
    in_specs = (
        P("brick", None, None),
        P(),
        P(),
        P(),
        P(),
        P("view"),
        P("view", "brick", None, None),
        P("view", None, "brick"),
    )
    out_specs = (P("view", None, "brick"), P("brick", None, None), P(), P(), P(), P())
    return jax.shard_map(body, mesh=mesh, in_specs=in_specs, out_specs=out_specs, check_vma=False)
```

```python
import functools

import jax
import jax.numpy as jnp
from jax import lax
from jax.experimental import pallas as pl
from jax.experimental.pallas import tpu as pltpu
from jax.sharding import PartitionSpec as P


F32 = jnp.float32
BF16 = jnp.bfloat16
NT = (((1,), (1,)), ((), ()))
STEPS = 8
TILE = 512
LANES = 128
PARTS = TILE // LANES
OUT_ROWS = 40


def mm(a, b):
    return jnp.dot(a, b, preferred_element_type=F32)


def mm_nt(a, b):
    return lax.dot_general(a, b, NT, preferred_element_type=F32)


def place_to_tile(place, brick):
    return jnp.bitwise_xor(jnp.bitwise_xor(place, jnp.right_shift(place, 2) * 2), brick)


def one_hot(local):
    low = jnp.bitwise_and(local, LANES - 1)
    rows = lax.broadcasted_iota(jnp.int32, (LANES, local.shape[1]), 0)
    return jnp.where(rows == low, 1.0, 0.0).astype(BF16)


def row_of(array, step):
    return array[step : step + 1, :]


def forward_kernel(
    first, brick_ref, grid_ref, samples_ref, one_ref, two_ref, three_ref, four_ref,
    partial_ref, trans_ref, hidden_ref, feature_ref, colour_ref, ray_ref, last_ref,
):
    tile = place_to_tile(pl.program_id(0) + first, brick_ref[0])
    spacing = 2.0 / (STEPS * 8)
    channels = grid_ref.shape[0]
    row = pl.program_id(0)
    for step in range(STEPS):
        span = pl.ds(step * TILE, TILE)
        local = jnp.bitwise_and(samples_ref[step : step + 1, :], TILE - 1)
        base = step * (grid_ref.shape[1] // STEPS) + tile * TILE
        pieces = [
            grid_ref[:, pl.ds(pl.multiple_of(base + k * LANES, LANES), LANES)]
            for k in range(PARTS)
        ]
        wide = mm(jnp.concatenate(pieces, axis=0), one_hot(local))
        high = jnp.broadcast_to(jnp.right_shift(local, 7), (channels, TILE))
        picked = wide[:channels]
        for k in range(1, PARTS):
            picked = jnp.where(high == k, wide[k * channels : (k + 1) * channels], picked)
        feature_ref[0, :, span] = picked.astype(BF16)
    for layer, weight_ref in enumerate((one_ref, two_ref, three_ref)):
        for step in range(STEPS):
            span = pl.ds(step * TILE, TILE)
            value = feature_ref[0, :, span] if layer == 0 else hidden_ref[0, layer - 1, :, span]
            half = mm(weight_ref[...] * 0.5, value)
            gate = 1.0 + jnp.tanh(half)
            hidden = half * gate
            hidden_ref[0, layer, :, span] = hidden.astype(BF16)
            hidden_ref[0, 3 + layer, :, span] = (gate + hidden * (2.0 - gate)).astype(BF16)
    for step in range(STEPS):
        span = pl.ds(step * TILE, TILE)
        output = mm(four_ref[...] * 0.5, hidden_ref[0, 2, :, span])
        colour_ref[0, :, span] = 0.5 + 0.5 * jnp.tanh(output[:32])
        last_ref[step : step + 1, :] = output[32:33]
    half = last_ref[...]
    raw = half + half
    depth = (jnp.maximum(raw, 0.0) + jnp.log1p(jnp.exp(-jnp.abs(raw)))) * spacing
    running = [row_of(depth, 0)]
    for step in range(1, STEPS):
        running.append(running[-1] + row_of(depth, step))
    earlier = jnp.concatenate([jnp.zeros_like(running[0])] + running[:-1], axis=0)
    running = jnp.concatenate(running, axis=0)
    through = jnp.exp(-running)
    small = depth * (1.0 - depth * (0.5 - depth * (1.0 / 6.0 - depth * (1.0 / 24.0))))
    absorbed = jnp.where(depth < 0.02, small, 1.0 - jnp.exp(-depth))
    factor = jnp.exp(-earlier) * absorbed
    ray_ref[0, 0] = factor
    ray_ref[0, 1] = through
    ray_ref[0, 2] = spacing * (0.5 + 0.5 * jnp.tanh(half))
    image = row_of(factor, 0) * colour_ref[0, :, 0:TILE]
    for step in range(1, STEPS):
        image = image + row_of(factor, step) * colour_ref[0, :, step * TILE : (step + 1) * TILE]
    partial_ref[0] = image
    trans_ref[pl.ds(row, 1), :] = through[STEPS - 1 : STEPS, :]


def backward_kernel(
    first, brick_ref, samples_ref, given_ref, weight_ref, behind_ref, hidden_ref, feature_ref,
    colour_ref, ray_ref, one_ref, two_ref, three_ref, four_ref, before_ref,
    grid_ref, packed_ref, cot_ref, out_ref, one_t_ref, mid_t_ref, four_t_ref,
):
    place = pl.program_id(0) + first
    channels = feature_ref.shape[1]

    @pl.when(pl.program_id(0) == 0)
    def _():
        packed_ref[...] = before_ref[...]
        one_t_ref[...] = (one_ref[...].astype(F32) * 0.5).T.astype(BF16)
        mid_t_ref[0] = (two_ref[...].astype(F32) * 0.5).T.astype(BF16)
        mid_t_ref[1] = (three_ref[...].astype(F32) * 0.5).T.astype(BF16)
        four = four_ref[...].astype(F32)
        padding = jnp.zeros((OUT_ROWS - four.shape[0], four.shape[1]), F32)
        four_t_ref[...] = jnp.concatenate([four, padding], axis=0).T.astype(BF16)

    weight = weight_ref[pl.ds(place, 1), :]
    trans_grad = weight * behind_ref[pl.ds(place, 1), :]
    factor = ray_ref[0, 0]
    through = ray_ref[0, 1]
    scaled = weight * given_ref[0]
    dots = jnp.concatenate(
        [
            jnp.sum(scaled * colour_ref[0, :, step * TILE : (step + 1) * TILE], axis=0, keepdims=True)
            for step in range(STEPS)
        ],
        axis=0,
    )
    taken = factor * dots
    later = [row_of(through, STEPS - 1) * trans_grad]
    for step in range(STEPS - 1, 0, -1):
        later.append(later[-1] + row_of(taken, step))
    depth_grad = through * dots - jnp.concatenate(later[::-1], axis=0)
    last = depth_grad * ray_ref[0, 2]
    first_row = lax.broadcasted_iota(jnp.int32, (OUT_ROWS - 32, TILE), 0) == 0
    for step in range(STEPS):
        span = pl.ds(step * TILE, TILE)
        colour = colour_ref[0, :, step * TILE : (step + 1) * TILE]
        out_ref[:, span] = jnp.concatenate(
            [
                (colour - colour * colour) * (row_of(factor, step) * scaled),
                jnp.where(first_row, row_of(last, step), 0.0),
            ],
            axis=0,
        ).astype(BF16)
    sums = [0.0, 0.0, 0.0, 0.0]
    for layer in (2, 1, 0):
        for step in range(STEPS):
            span = pl.ds(step * TILE, TILE)
            weight_t = four_t_ref[...] if layer == 2 else mid_t_ref[layer]
            cot = out_ref[:, span] if layer == 2 else cot_ref[layer + 1, :, span]
            cot_ref[layer, :, span] = (
                mm(weight_t, cot).astype(BF16) * hidden_ref[0, 3 + layer, :, span]
            )
            if step % 2 == 1:
                pair = pl.ds((step - 1) * TILE, 2 * TILE)
                cot = out_ref[:, pair] if layer == 2 else cot_ref[layer + 1, :, pair]
                sums[layer + 1] += mm_nt(cot, hidden_ref[0, layer, :, pair])
    for step in range(STEPS):
        span = pl.ds(step * TILE, TILE)
        feature_cot = mm(one_t_ref[...], cot_ref[0, :, span]).astype(BF16).astype(F32)
        local = jnp.bitwise_and(samples_ref[step : step + 1, :], TILE - 1)
        high = jnp.broadcast_to(jnp.right_shift(local, 7), (channels, TILE))
        spread = jnp.concatenate(
            [jnp.where(high == k, feature_cot, 0.0) for k in range(PARTS)], axis=0
        ).astype(BF16)
        grid_ref[0, step] = mm_nt(spread, one_hot(local))
        if step % 2 == 1:
            pair = pl.ds((step - 1) * TILE, 2 * TILE)
            sums[0] += mm_nt(feature_ref[0, :, pair], cot_ref[0, :, pair])

    packed_ref[0:64, 0:64] += 0.5 * sums[1]
    packed_ref[0:64, 64:128] += 0.5 * sums[2]
    packed_ref[64:104, 0:64] += sums[3]
    packed_ref[64:80, 64:128] += 0.5 * sums[0]


def finish_kernel(info_ref, *refs):
    halves, (packed_in_ref, grid_ref, one_ref, two_ref, three_ref, four_ref) = refs[:8], refs[8:]
    channels = grid_ref.shape[1]
    slab = grid_ref.shape[2] // STEPS
    for colour in range(4):
        for which in range(2):
            bit = info_ref[1 + colour]
            place = 2 * colour + (bit if which == 0 else 1 - bit)
            tile = place_to_tile(place, info_ref[0])
            source = halves[2 * colour + which]
            for step in range(STEPS):
                for k in range(PARTS):
                    base = step * slab + tile * TILE + k * LANES
                    grid_ref[0, :, pl.ds(pl.multiple_of(base, LANES), LANES)] = source[
                        step, k * channels : (k + 1) * channels, :
                    ]
    one_ref[...] = packed_in_ref[64:80, 64:128].T
    two_ref[...] = packed_in_ref[0:64, 0:64]
    three_ref[...] = packed_in_ref[0:64, 64:128]
    four_ref[...] = packed_in_ref[64:97, 0:64]


def whole(shape):
    return pl.BlockSpec(shape, lambda p, brick: (0,) * len(shape))


def at_place(shape):
    return pl.BlockSpec((1,) + shape, lambda p, brick: (p,) + (0,) * len(shape))


def run_forward(first, brick, grid, samples, one, two, three, four):
    count = 4
    wide = STEPS * TILE
    channels = grid.shape[0]
    shapes = [
        jax.ShapeDtypeStruct((count, 32, TILE), F32),
        jax.ShapeDtypeStruct((count, TILE), F32),
        jax.ShapeDtypeStruct((count, 6, 64, wide), BF16),
        jax.ShapeDtypeStruct((count, channels, wide), BF16),
        jax.ShapeDtypeStruct((count, 32, wide), F32),
        jax.ShapeDtypeStruct((count, 3, STEPS, TILE), F32),
    ]
    return pl.pallas_call(
        functools.partial(forward_kernel, first),
        out_shape=shapes,
        grid_spec=pltpu.PrefetchScalarGridSpec(
            num_scalar_prefetch=1,
            grid=(count,),
            in_specs=[
                whole(grid.shape),
                pl.BlockSpec(
                    (STEPS, TILE), lambda p, brick: (0, place_to_tile(p + first, brick[0]))
                ),
                whole(one.shape),
                whole(two.shape),
                whole(three.shape),
                whole(four.shape),
            ],
            out_specs=[
                at_place((32, TILE)),
                whole((count, TILE)),
                at_place((6, 64, wide)),
                at_place((channels, wide)),
                at_place((32, wide)),
                at_place((3, STEPS, TILE)),
            ],
            scratch_shapes=[pltpu.VMEM((STEPS, TILE), F32)],
        ),
        cost_estimate=pl.CostEstimate(
            flops=1_000_000_000, bytes_accessed=16_000_000, transcendentals=4_000_000
        ),
        name="forward",
    )(brick, grid, samples, one, two, three, four)


def run_backward(first, brick, samples, given, weight, behind, saved, layers, before):
    count = 2
    skip = first % 4
    wide = STEPS * TILE
    hidden, feature, colour, ray = saved
    channels = feature.shape[1]

    def later(shape):
        return pl.BlockSpec((1,) + shape, lambda p, brick: (p + skip,) + (0,) * len(shape))

    return pl.pallas_call(
        functools.partial(backward_kernel, first),
        out_shape=[
            jax.ShapeDtypeStruct((count, STEPS, PARTS * channels, LANES), F32),
            jax.ShapeDtypeStruct((104, 128), F32),
        ],
        grid_spec=pltpu.PrefetchScalarGridSpec(
            num_scalar_prefetch=1,
            grid=(count,),
            in_specs=[
                pl.BlockSpec(
                    (STEPS, TILE), lambda p, brick: (0, place_to_tile(p + first, brick[0]))
                ),
                later((32, TILE)),
                whole(weight.shape),
                whole(behind.shape),
                later((6, 64, wide)),
                later((channels, wide)),
                later((32, wide)),
                later((3, STEPS, TILE)),
                *[whole(layer.shape) for layer in layers],
                whole((104, 128)),
            ],
            out_specs=[
                at_place((STEPS, PARTS * channels, LANES)),
                whole((104, 128)),
            ],
            scratch_shapes=[
                pltpu.VMEM((3, 64, wide), BF16),
                pltpu.VMEM((OUT_ROWS, wide), BF16),
                pltpu.VMEM((channels, 64), BF16),
                pltpu.VMEM((2, 64, 64), BF16),
                pltpu.VMEM((64, OUT_ROWS), BF16),
            ],
        ),
        cost_estimate=pl.CostEstimate(
            flops=1_000_000_000, bytes_accessed=9_000_000, transcendentals=0
        ),
        name="backward",
    )(brick, samples, given, weight, behind, hidden, feature, colour, ray, *layers, before)


def run_finish(info, halves, packed, voxels):
    channels = halves[0].shape[1] // PARTS
    vmem = pl.BlockSpec(memory_space=pltpu.VMEM)
    return pl.pallas_call(
        finish_kernel,
        out_shape=[
            jax.ShapeDtypeStruct((1, channels, voxels), F32),
            jax.ShapeDtypeStruct((64, channels), F32),
            jax.ShapeDtypeStruct((64, 64), F32),
            jax.ShapeDtypeStruct((64, 64), F32),
            jax.ShapeDtypeStruct((33, 64), F32),
        ],
        in_specs=[pl.BlockSpec(memory_space=pltpu.SMEM)] + [vmem] * 9,
        out_specs=[vmem] * 5,
        name="finish",
    )(info, *halves, packed)


def swap_brick(array, flip):
    return lax.ppermute(array, "brick", [(i, i ^ flip) for i in range(8)])


def swap_rows(array, flip):
    parts = array.reshape((8 // (2 * flip), 2, flip) + array.shape[1:])
    return jnp.flip(parts, axis=1).reshape(array.shape)


def view_swap(array, dim):
    pairs = []
    for view in range(16):
        y, x = view // 4, view % 4
        for brick in range(8):
            at = (dim + 2 * (brick % 2)) % 4
            flip = 1 if at < 2 else 3
            other = y * 4 + (x ^ flip) if at % 2 == 0 else (y ^ flip) * 4 + x
            pairs.append((brick * 16 + view, brick * 16 + other))
    return lax.ppermute(array, ("brick", "view"), pairs)


def view_bits(brick):
    view = lax.axis_index("view")
    y = view // 4
    x = view % 4
    bits = [
        jnp.bitwise_and(x ^ (x >> 1), 1),
        jnp.bitwise_and(y ^ (y >> 1), 1),
        x >> 1,
        y >> 1,
    ]
    odd = jnp.bitwise_and(brick, 1) == 1
    return [jnp.where(odd, bits[(dim + 2) % 4], bits[dim]) for dim in range(4)]


def pick(array, index):
    return lax.dynamic_index_in_dim(array, index, 0, False)


def body(
    latent_grid, layer_one, layer_two, layer_three, layer_four, view_order, samples, pixel_grad
):
    brick_id = lax.axis_index("brick")
    rank = jnp.bitwise_xor(brick_id, view_order[0])
    brick = jnp.reshape(brick_id, (1,)).astype(jnp.int32)
    voxels = latent_grid.shape[2]
    index = samples[0, 0]
    layers = (layer_one, layer_two, layer_three, layer_four)
    bits = view_bits(brick_id)

    near = pixel_grad
    for flip in (1, 2):
        near = jnp.concatenate([near, swap_brick(near, flip)], axis=0)
    part_near, trans_near, *saved_near = run_forward(0, brick, latent_grid[0], index, *layers)
    far = swap_brick(near, 6)
    part_far, trans_far, *saved_far = run_forward(4, brick, latent_grid[0], index, *layers)

    total = jnp.concatenate([trans_near, trans_far], axis=0)
    dots = jnp.concatenate(
        [jnp.sum(part_near * near, axis=1), jnp.sum(part_far * far, axis=1)], axis=0
    )
    front, after, behind = jnp.ones_like(total), jnp.ones_like(total), jnp.zeros_like(total)
    for level, (flip, rows) in enumerate(((1, 1), (2, 2), (6, 4))):
        got = swap_brick(jnp.stack([total, dots]), flip)
        got_total = swap_rows(got[0], rows)
        got_dots = swap_rows(got[1], rows)
        first = jnp.bitwise_and(jnp.right_shift(rank, level), 1) == 0
        behind = jnp.where(first, behind + after * got_dots, behind)
        after = jnp.where(first, after * got_total, after)
        front = jnp.where(first, front, front * got_total)
        dots = jnp.where(first, dots + total * got_dots, got_dots + got_total * dots)
        total = total * got_total

    image = front[:4, None, :] * part_near + swap_brick(front[4:, None, :] * part_far, 6)
    for flip, keep in ((2, 2), (1, 1)):
        image = image[:keep] + swap_brick(image[keep:], flip)

    packed = jnp.zeros((104, 128), F32)
    parts = []
    for c in range(4):
        given, saved = (near, saved_near) if c < 2 else (far, saved_far)
        grid, packed = run_backward(
            2 * c, brick, index, given, front, behind, saved, layers, packed
        )
        parts.append(grid.reshape((2, 2, 4) + grid.shape[2:]))
    for flip in (1, 2, 6):
        packed = packed + swap_brick(packed, flip)

    def carried(array, extra, dim):
        rows = array.size // LANES
        sent = jnp.concatenate([array.reshape(rows, LANES), extra], axis=0)
        got = view_swap(sent, dim)
        return got[:rows].reshape(array.shape), extra + got[rows:]

    halves = []
    for c in range(4):
        dims = [(c + turn) % 4 for turn in range(4)]
        part = parts[c]
        for dim in dims[:2]:
            part = pick(part, bits[dim]) + view_swap(pick(part, 1 - bits[dim]), dim)
        for dim in dims[2:]:
            if c == 3:
                got, packed = carried(part, packed, dim)
            else:
                got = view_swap(part, dim)
            part = part + got
        if c == 3:
            got, packed = carried(part, packed, dims[1])
        else:
            got = view_swap(part, dims[1])
        part = jnp.where(bits[dims[1]] == 0, jnp.stack([part, got]), jnp.stack([got, part]))
        if c == 3:
            got, packed = carried(part, packed, dims[0])
        else:
            got = view_swap(part, dims[0])
        halves += [part.reshape((STEPS,) + part.shape[2:]), got.reshape((STEPS,) + got.shape[2:])]

    info = jnp.stack([brick_id] + [bits[c] for c in range(4)]).astype(jnp.int32)
    grid, one, two, three, four = run_finish(info, halves, packed, voxels)
    return (image, grid, one, two, three, four)


def solution(mesh):
    in_specs = (
        P("brick", None, None),
        P(),
        P(),
        P(),
        P(),
        P("view"),
        P("view", "brick", None, None),
        P("view", None, "brick"),
    )
    out_specs = (P("view", None, "brick"), P("brick", None, None), P(), P(), P(), P())
    return jax.shard_map(body, mesh=mesh, in_specs=in_specs, out_specs=out_specs, check_vma=False)
```

```python
import functools

import jax
import jax.numpy as jnp
from jax import lax
from jax.experimental import pallas as pl
from jax.experimental.pallas import tpu as pltpu
from jax.sharding import PartitionSpec as P


F32 = jnp.float32
BF16 = jnp.bfloat16
NT = (((1,), (1,)), ((), ()))
STEPS = 8
TILE = 512
LANES = 128
PARTS = TILE // LANES
OUT_ROWS = 40


def mm(a, b):
    return jnp.dot(a, b, preferred_element_type=F32)


def mm_nt(a, b):
    return lax.dot_general(a, b, NT, preferred_element_type=F32)


def place_to_tile(place, brick):
    return jnp.bitwise_xor(jnp.bitwise_xor(place, jnp.right_shift(place, 2) * 2), brick)


def one_hot(local):
    low = jnp.bitwise_and(local, LANES - 1)
    rows = lax.broadcasted_iota(jnp.int32, (LANES, local.shape[1]), 0)
    return jnp.where(rows == low, 1.0, 0.0).astype(BF16)


def row_of(array, step):
    return array[step : step + 1, :]


def colour_at(colour_ref, step):
    return colour_ref[0, :, step * TILE : (step + 1) * TILE].astype(F32)


def forward_kernel(
    first, brick_ref, grid_ref, samples_ref, one_ref, two_ref, three_ref, four_ref,
    partial_ref, trans_ref, hidden_ref, feature_ref, colour_ref, ray_ref, last_ref,
):
    tile = place_to_tile(pl.program_id(0) + first, brick_ref[0])
    spacing = 2.0 / (STEPS * 8)
    channels = grid_ref.shape[0]
    row = pl.program_id(0)
    for step in range(STEPS):
        span = pl.ds(step * TILE, TILE)
        local = jnp.bitwise_and(samples_ref[step : step + 1, :], TILE - 1)
        base = step * (grid_ref.shape[1] // STEPS) + tile * TILE
        pieces = [
            grid_ref[:, pl.ds(pl.multiple_of(base + k * LANES, LANES), LANES)]
            for k in range(PARTS)
        ]
        wide = mm(jnp.concatenate(pieces, axis=0), one_hot(local))
        high = jnp.broadcast_to(jnp.right_shift(local, 7), (channels, TILE))
        picked = wide[:channels]
        for k in range(1, PARTS):
            picked = jnp.where(high == k, wide[k * channels : (k + 1) * channels], picked)
        feature_ref[0, :, span] = picked.astype(BF16)
    for layer, weight_ref in enumerate((one_ref, two_ref, three_ref)):
        for step in range(STEPS):
            span = pl.ds(step * TILE, TILE)
            value = feature_ref[0, :, span] if layer == 0 else hidden_ref[0, layer - 1, :, span]
            half = mm(weight_ref[...], value)
            gate = 1.0 + jnp.tanh(half)
            hidden = half * gate
            hidden = hidden.astype(BF16)
            gate = gate.astype(BF16)
            hidden_ref[0, layer, :, span] = hidden
            hidden_ref[0, 3 + layer, :, span] = gate + hidden * (2.0 - gate)
    for step in range(STEPS):
        span = pl.ds(step * TILE, TILE)
        output = mm(four_ref[...], hidden_ref[0, 2, :, span])
        colour_ref[0, :, span] = (0.5 + 0.5 * jnp.tanh(output[:32])).astype(BF16)
        last_ref[step : step + 1, :] = output[32:33]
    half = last_ref[...]
    raw = half + half
    depth = (jnp.maximum(raw, 0.0) + jnp.log1p(jnp.exp(-jnp.abs(raw)))) * spacing
    running = [row_of(depth, 0)]
    for step in range(1, STEPS):
        running.append(running[-1] + row_of(depth, step))
    earlier = jnp.concatenate([jnp.zeros_like(running[0])] + running[:-1], axis=0)
    running = jnp.concatenate(running, axis=0)
    through = jnp.exp(-running)
    small = depth * (1.0 - depth * (0.5 - depth * (1.0 / 6.0 - depth * (1.0 / 24.0))))
    absorbed = jnp.where(depth < 0.02, small, 1.0 - jnp.exp(-depth))
    factor = jnp.exp(-earlier) * absorbed
    ray_ref[0, 0] = factor
    ray_ref[0, 1] = through
    ray_ref[0, 2] = spacing * (0.5 + 0.5 * jnp.tanh(half))
    image = row_of(factor, 0) * colour_at(colour_ref, 0)
    for step in range(1, STEPS):
        image = image + row_of(factor, step) * colour_at(colour_ref, step)
    partial_ref[0] = image
    trans_ref[pl.ds(row, 1), :] = through[STEPS - 1 : STEPS, :]


def backward_kernel(
    first, brick_ref, samples_ref, given_ref, weight_ref, behind_ref, hidden_ref, feature_ref,
    colour_ref, ray_ref, one_t_ref, two_t_ref, three_t_ref, four_t_ref, before_ref,
    grid_ref, packed_ref, cot_ref, out_ref, feature_cot_ref,
):
    place = pl.program_id(0) + first
    channels = feature_ref.shape[1]

    @pl.when(pl.program_id(0) == 0)
    def _():
        if first == 0:
            packed_ref[...] = jnp.zeros_like(packed_ref)
        else:
            packed_ref[...] = before_ref[...]

    weight = weight_ref[pl.ds(place, 1), :]
    trans_grad = weight * behind_ref[pl.ds(place, 1), :]
    factor = ray_ref[0, 0]
    through = ray_ref[0, 1]
    scaled = weight * given_ref[0]
    dots = jnp.concatenate(
        [
            jnp.sum(scaled * colour_at(colour_ref, step), axis=0, keepdims=True)
            for step in range(STEPS)
        ],
        axis=0,
    )
    taken = factor * dots
    later = [row_of(through, STEPS - 1) * trans_grad]
    for step in range(STEPS - 1, 0, -1):
        later.append(later[-1] + row_of(taken, step))
    depth_grad = through * dots - jnp.concatenate(later[::-1], axis=0)
    last = depth_grad * ray_ref[0, 2]
    first_row = lax.broadcasted_iota(jnp.int32, (OUT_ROWS - 32, TILE), 0) == 0
    for step in range(STEPS):
        span = pl.ds(step * TILE, TILE)
        colour = colour_at(colour_ref, step)
        out_ref[:, span] = jnp.concatenate(
            [
                (colour - colour * colour) * (row_of(factor, step) * scaled),
                jnp.where(first_row, row_of(last, step), 0.0),
            ],
            axis=0,
        ).astype(BF16)
    sums = [0.0] * 4
    for layer in (2, 1, 0):
        for step in range(STEPS):
            span = pl.ds(step * TILE, TILE)
            weight_t = (two_t_ref, three_t_ref, four_t_ref)[layer][...]
            cot = out_ref[:, span] if layer == 2 else cot_ref[layer + 1, :, span]
            cot_ref[layer, :, span] = (
                mm(weight_t, cot).astype(BF16) * hidden_ref[0, 3 + layer, :, span]
            )
            if step % 2 == 1:
                pair = pl.ds((step - 1) * TILE, 2 * TILE)
                cot = out_ref[:, pair] if layer == 2 else cot_ref[layer + 1, :, pair]
                sums[layer + 1] += mm_nt(cot, hidden_ref[0, layer, :, pair])
    for step in range(STEPS):
        span = pl.ds(step * TILE, TILE)
        feature_cot_ref[:, span] = mm(one_t_ref[...], cot_ref[0, :, span]).astype(BF16)
        if step % 2 == 1:
            pair = pl.ds((step - 1) * TILE, 2 * TILE)
            sums[0] += mm_nt(feature_ref[0, :, pair], cot_ref[0, :, pair])
    for step in range(STEPS):
        feature_cot = feature_cot_ref[:, pl.ds(step * TILE, TILE)].astype(F32)
        local = jnp.bitwise_and(samples_ref[step : step + 1, :], TILE - 1)
        high = jnp.broadcast_to(jnp.right_shift(local, 7), (channels, TILE))
        spread = jnp.concatenate(
            [jnp.where(high == k, feature_cot, 0.0) for k in range(PARTS)], axis=0
        ).astype(BF16)
        half = jnp.bitwise_xor(step // 4, brick_ref[6 + first // 2])
        grid_ref[0, half * 4 + step % 4] = mm_nt(spread, one_hot(local))

    for half in range(2):
        rows = slice(32 * half, 32 * half + 32)
        packed_ref[0, :, 128 * half : 128 * half + 64] += 0.5 * sums[1][rows]
        packed_ref[0, :, 128 * half + 64 : 128 * half + 128] += 0.5 * sums[2][rows]
    packed_ref[0, :, 256:320] += sums[3][0:32]
    packed_ref[0, 0:8, 384:448] += sums[3][32:40]
    packed_ref[0, 0:16, 320:384] += 0.5 * sums[0]


def prepare_kernel(
    grid_in_ref, samples_in_ref, one_t_in_ref, two_in_ref, three_in_ref, four_in_ref,
    grid_ref, samples_ref, one_ref, two_ref, three_ref, four_ref,
    one_t_ref, two_t_ref, three_t_ref, four_t_ref,
):
    grid_ref[...] = grid_in_ref[...]
    samples_ref[...] = samples_in_ref[...]
    one_t = one_t_in_ref[...].astype(F32) * 0.5
    one_ref[...] = one_t.T.astype(BF16)
    one_t_ref[...] = one_t.astype(BF16)
    for in_ref, plain_ref, turned_ref in (
        (two_in_ref, two_ref, two_t_ref),
        (three_in_ref, three_ref, three_t_ref),
    ):
        layer = in_ref[...].astype(F32) * 0.5
        plain_ref[...] = layer.astype(BF16)
        turned_ref[...] = layer.T.astype(BF16)
    four = four_in_ref[...].astype(F32)
    four = jnp.concatenate([four, jnp.zeros((OUT_ROWS - four.shape[0], 64), F32)], axis=0)
    four_ref[...] = (four * 0.5).astype(BF16)
    four_t_ref[...] = four.T.astype(BF16)


def flip_rows(array, flip):
    if flip == 4:
        return pltpu.roll(array, 4, 0)
    rows = lax.broadcasted_iota(jnp.int32, array.shape, 0)
    upper = jnp.bitwise_and(rows, flip) == 0
    return jnp.where(upper, pltpu.roll(array, 8 - flip, 0), pltpu.roll(array, flip, 0))


def dots_kernel(near_ref, far_ref, part_near_ref, part_far_ref, trans_near_ref, trans_far_ref, out_ref):
    out_ref[0, 0:4, :] = trans_near_ref[...]
    out_ref[0, 4:8, :] = trans_far_ref[...]
    for half, (given_ref, part_ref) in enumerate(
        ((near_ref, part_near_ref), (far_ref, part_far_ref))
    ):
        for p in range(4):
            row = 4 * half + p
            out_ref[1, row : row + 1, :] = jnp.sum(
                given_ref[p] * part_ref[p], axis=0, keepdims=True
            )


def merge_kernel(level, flip, info_ref, own_ref, got_ref, *refs):
    total, dots = own_ref[0], own_ref[1]
    got_total = flip_rows(got_ref[0], flip)
    got_dots = flip_rows(got_ref[1], flip)
    bit = jnp.bitwise_and(jnp.right_shift(info_ref[1], level), 1)
    first = jnp.full(total.shape, bit, jnp.int32) == 0
    if level == 0:
        front, after, behind = jnp.ones_like(total), jnp.ones_like(total), jnp.zeros_like(total)
    else:
        state_ref, *refs = refs
        front, after, behind = state_ref[0], state_ref[1], state_ref[2]
    behind = jnp.where(first, behind + after * got_dots, behind)
    front = jnp.where(first, front, front * got_total)
    if level < 2:
        out_ref, next_ref = refs
        next_ref[0] = front
        next_ref[1] = jnp.where(first, after * got_total, after)
        next_ref[2] = behind
        out_ref[0] = total * got_total
        out_ref[1] = jnp.where(first, dots + total * got_dots, got_dots + got_total * dots)
    else:
        part_near_ref, part_far_ref, front_ref, behind_ref, image_near_ref, image_far_ref = refs
        front_ref[...] = front
        behind_ref[...] = behind
        for p in range(4):
            image_near_ref[p] = front[p : p + 1] * part_near_ref[p]
            image_far_ref[p] = front[p + 4 : p + 5] * part_far_ref[p]


def finish_kernel(info_ref, *refs):
    sources, (packed_in_ref, grid_ref, one_t_ref, two_ref, three_ref, four_ref) = refs[:12], refs[12:]
    channels = grid_ref.shape[1]
    slab = grid_ref.shape[2] // STEPS

    rows = 4 * PARTS * channels
    for colour in range(4):
        bit = info_ref[2 + colour]
        for part in range(4):
            source = sources[3 * colour + min(part, 2)]
            skip = rows if part == 3 else 0
            tile = place_to_tile(2 * colour + jnp.bitwise_xor(bit, part // 2), info_ref[0])
            half = jnp.bitwise_xor(info_ref[6 + colour], part % 2)
            for step in range(4):
                for k in range(PARTS):
                    base = (half * 4 + step) * slab + tile * TILE + k * LANES
                    row = skip + (step * PARTS + k) * channels
                    grid_ref[0, :, pl.ds(pl.multiple_of(base, LANES), LANES)] = source[
                        row : row + channels, :
                    ]
    packed_in_ref = packed_in_ref[...] + sources[11][2 * rows :, :]
    one_t_ref[...] = packed_in_ref[64:80, 64:128]
    two_ref[...] = packed_in_ref[0:64, 0:64]
    three_ref[...] = packed_in_ref[0:64, 64:128]
    four_ref[...] = packed_in_ref[64:97, 0:64]


VMEM = pl.BlockSpec(memory_space=pltpu.VMEM)
SMEM = pl.BlockSpec(memory_space=pltpu.SMEM)
SMALL = pltpu.CompilerParams(vmem_limit_bytes=4 * 2**20)


def run_prepare(grid, samples, one_t, two, three, four):
    channels = one_t.shape[0]
    shapes = [(64, channels), (64, 64), (64, 64), (OUT_ROWS, 64)]
    shapes += [shape[::-1] for shape in shapes]
    return pl.pallas_call(
        prepare_kernel,
        out_shape=[
            jax.ShapeDtypeStruct(grid.shape, grid.dtype),
            jax.ShapeDtypeStruct(samples.shape, samples.dtype),
            *[jax.ShapeDtypeStruct(shape, BF16) for shape in shapes],
        ],
        in_specs=[VMEM] * 6,
        out_specs=[VMEM] * 10,
        compiler_params=SMALL,
        name="prepare",
    )(grid, samples, one_t, two, three, four)


def run_dots(*arrays):
    return pl.pallas_call(
        dots_kernel,
        out_shape=jax.ShapeDtypeStruct((2, 8, TILE), F32),
        in_specs=[VMEM] * 6,
        out_specs=VMEM,
        compiler_params=SMALL,
        name="dots",
    )(*arrays)


def run_merge(level, flip, info, own, got, *more):
    shapes = {
        False: [(2, 8, TILE), (3, 8, TILE)],
        True: [(8, TILE), (8, TILE), (4, 32, TILE), (4, 32, TILE)],
    }[level == 2]
    return pl.pallas_call(
        functools.partial(merge_kernel, level, flip),
        out_shape=[jax.ShapeDtypeStruct(shape, F32) for shape in shapes],
        in_specs=[SMEM] + [VMEM] * (2 + len(more)),
        out_specs=[VMEM] * len(shapes),
        compiler_params=SMALL,
        name="merge",
    )(info, own, got, *more)


def whole(shape):
    return pl.BlockSpec(shape, lambda p, brick: (0,) * len(shape))


def at_place(shape):
    return pl.BlockSpec((1,) + shape, lambda p, brick: (p,) + (0,) * len(shape))


def run_forward(first, brick, grid, samples, one, two, three, four):
    count = 4
    wide = STEPS * TILE
    channels = grid.shape[0]
    shapes = [
        jax.ShapeDtypeStruct((count, 32, TILE), F32),
        jax.ShapeDtypeStruct((count, TILE), F32),
        jax.ShapeDtypeStruct((count, 6, 64, wide), BF16),
        jax.ShapeDtypeStruct((count, channels, wide), BF16),
        jax.ShapeDtypeStruct((count, 32, wide), BF16),
        jax.ShapeDtypeStruct((count, 3, STEPS, TILE), F32),
    ]
    return pl.pallas_call(
        functools.partial(forward_kernel, first),
        out_shape=shapes,
        grid_spec=pltpu.PrefetchScalarGridSpec(
            num_scalar_prefetch=1,
            grid=(count,),
            in_specs=[
                whole(grid.shape),
                pl.BlockSpec(
                    (STEPS, TILE), lambda p, brick: (0, place_to_tile(p + first, brick[0]))
                ),
                whole(one.shape),
                whole(two.shape),
                whole(three.shape),
                whole(four.shape),
            ],
            out_specs=[
                at_place((32, TILE)),
                whole((count, TILE)),
                at_place((6, 64, wide)),
                at_place((channels, wide)),
                at_place((32, wide)),
                at_place((3, STEPS, TILE)),
            ],
            scratch_shapes=[pltpu.VMEM((STEPS, TILE), F32)],
        ),
        cost_estimate=pl.CostEstimate(
            flops=1_000_000_000, bytes_accessed=16_000_000, transcendentals=4_000_000
        ),
        compiler_params=pltpu.CompilerParams(vmem_limit_bytes=14 * 2**20),
        name="forward",
    )(brick, grid, samples, one, two, three, four)


def run_backward(first, brick, samples, given, weight, behind, saved, layers, before):
    count = 2
    skip = first % 4
    wide = STEPS * TILE
    hidden, feature, colour, ray = saved
    channels = feature.shape[1]

    def later(shape):
        return pl.BlockSpec((1,) + shape, lambda p, brick: (p + skip,) + (0,) * len(shape))

    return pl.pallas_call(
        functools.partial(backward_kernel, first),
        out_shape=[
            jax.ShapeDtypeStruct((count, STEPS, PARTS * channels, LANES), F32),
            jax.ShapeDtypeStruct((1, 32, TILE), F32),
        ],
        grid_spec=pltpu.PrefetchScalarGridSpec(
            num_scalar_prefetch=1,
            grid=(count,),
            in_specs=[
                pl.BlockSpec(
                    (STEPS, TILE), lambda p, brick: (0, place_to_tile(p + first, brick[0]))
                ),
                later((32, TILE)),
                whole(weight.shape),
                whole(behind.shape),
                later((6, 64, wide)),
                later((channels, wide)),
                later((32, wide)),
                later((3, STEPS, TILE)),
                *[whole(layer.shape) for layer in layers],
                whole((1, 32, TILE)),
            ],
            out_specs=[
                pl.BlockSpec(
                    (1, STEPS, PARTS * channels, LANES),
                    lambda p, brick: (jnp.bitwise_xor(p, brick[2 + first // 2]), 0, 0, 0),
                ),
                whole((1, 32, TILE)),
            ],
            scratch_shapes=[
                pltpu.VMEM((3, 64, wide), BF16),
                pltpu.VMEM((OUT_ROWS, wide), BF16),
                pltpu.VMEM((channels, wide), BF16),
            ],
        ),
        cost_estimate=pl.CostEstimate(
            flops=1_000_000_000, bytes_accessed=9_000_000, transcendentals=0
        ),
        compiler_params=pltpu.CompilerParams(vmem_limit_bytes=14 * 2**20),
        name="backward",
    )(brick, samples, given, weight, behind, hidden, feature, colour, ray, *layers, before)


def run_finish(info, sources, packed, channels, voxels):
    return pl.pallas_call(
        finish_kernel,
        out_shape=[
            jax.ShapeDtypeStruct((1, channels, voxels), F32),
            jax.ShapeDtypeStruct((channels, 64), F32),
            jax.ShapeDtypeStruct((64, 64), F32),
            jax.ShapeDtypeStruct((64, 64), F32),
            jax.ShapeDtypeStruct((33, 64), F32),
        ],
        in_specs=[SMEM] + [VMEM] * 13,
        out_specs=[VMEM] * 5,
        compiler_params=pltpu.CompilerParams(vmem_limit_bytes=14 * 2**20),
        name="finish",
    )(info, *sources, packed)


def swap_brick(array, flip):
    return lax.ppermute(array, "brick", [(i, i ^ flip) for i in range(8)])


def link_of(colour, turn, odd):
    return (2 * colour + turn + 2 * odd) % 4


def view_swap(array, colour, turn):
    pairs = []
    for view in range(16):
        y, x = view // 4, view % 4
        for brick in range(8):
            dim = link_of(colour, turn, brick % 2)
            flip = 1 if dim < 2 else 3
            other = y * 4 + (x ^ flip) if dim % 2 == 0 else (y ^ flip) * 4 + x
            pairs.append((brick * 16 + view, brick * 16 + other))
    return lax.ppermute(array, ("brick", "view"), pairs)


def make_info(brick, rank):
    view = lax.axis_index("view")
    y = jnp.right_shift(view, 2)
    x = jnp.bitwise_and(view, 3)
    bits = [
        jnp.bitwise_and(x ^ (x >> 1), 1),
        jnp.bitwise_and(y ^ (y >> 1), 1),
        x >> 1,
        y >> 1,
    ]
    odd = jnp.bitwise_and(brick, 1) == 1
    values = [brick, rank]
    for turn in range(2):
        for colour in range(4):
            even_bit, odd_bit = (bits[link_of(colour, turn, at)] for at in range(2))
            values.append(jnp.where(odd, odd_bit, even_bit))
    return jnp.stack(values).astype(jnp.int32)


def work(
    latent_grid, layer_one, layer_two, layer_three, layer_four, view_order, samples, pixel_grad
):
    brick = lax.axis_index("brick")
    info = make_info(brick, jnp.bitwise_xor(brick, view_order[0]))
    voxels = latent_grid.shape[2]

    latent, index, *layers = run_prepare(
        *[
            pltpu.with_memory_space_constraint(array, pltpu.HBM)
            for array in (
                latent_grid[0], samples[0, 0], layer_one.T, layer_two, layer_three, layer_four,
            )
        ]
    )
    plain, turned = layers[:4], layers[4:]

    near = pixel_grad
    for flip in (1, 2):
        near = jnp.concatenate([near, swap_brick(near, flip)], axis=0)
    part_near, trans_near, *saved_near = run_forward(0, info, latent, index, *plain)
    far = swap_brick(near, 6)
    part_far, trans_far, *saved_far = run_forward(4, info, latent, index, *plain)

    own = run_dots(near, far, part_near, part_far, trans_near, trans_far)
    own, state = run_merge(0, 1, info, own, swap_brick(own, 1))
    own, state = run_merge(1, 2, info, own, swap_brick(own, 2), state)
    front, behind, image_near, image_far = run_merge(
        2, 4, info, own, swap_brick(own, 6), state, part_near, part_far
    )

    image = image_near + swap_brick(image_far, 6)
    image = image[:2] + swap_brick(image[2:], 2)
    image = image[:1] + swap_brick(image[1:], 1)

    packed = jnp.zeros((1, 32, TILE), F32)
    grids = []
    for colour in range(4):
        given, saved = (near, saved_near) if colour < 2 else (far, saved_far)
        grid, packed = run_backward(
            2 * colour, info, index, given, front, behind, saved, turned, packed
        )
        grids.append(grid.reshape((2, 2, 4) + grid.shape[2:]))
    for flip in (1, 2, 6):
        packed = packed + swap_brick(packed, flip)
    packed = jnp.concatenate([packed[0, :, k * LANES : (k + 1) * LANES] for k in range(4)], axis=0)
    packed = packed[:104]

    sources = []
    for colour in range(4):
        part = grids[colour]
        for turn in range(2):
            part = part[0] + view_swap(part[1], colour, turn)
        part = part.reshape(-1, LANES)
        rows = part.shape[0]
        if colour == 3:
            part = jnp.concatenate([part, packed], axis=0)
        for turn in (2, 3):
            part = part + view_swap(part, colour, turn)
        got = view_swap(part, colour, 1)
        sent = jnp.concatenate([part[:rows], got[:rows]], axis=0)
        if colour == 3:
            packed = part[rows:] + got[rows:]
            sent = jnp.concatenate([sent, packed], axis=0)
        sources += [part, got, view_swap(sent, colour, 0)]

    channels = latent_grid.shape[1]
    grid, one_t, two, three, four = run_finish(info, sources, packed, channels, voxels)
    return (image, grid, one_t.T, two, three, four)


def solution(mesh):
    in_specs = (
        P("brick", None, None),
        P(),
        P(),
        P(),
        P(),
        P("view"),
        P("view", "brick", None, None),
        P("view", None, "brick"),
    )
    out_specs = (P("view", None, "brick"), P("brick", None, None), P(), P(), P(), P())
    return jax.shard_map(work, mesh=mesh, in_specs=in_specs, out_specs=out_specs, check_vma=False)
```

```python
import functools

import jax
import jax.numpy as jnp
from jax import lax
from jax.experimental import pallas as pl
from jax.experimental.pallas import tpu as pltpu
from jax.sharding import PartitionSpec as P


F32 = jnp.float32
BF16 = jnp.bfloat16
NT = (((1,), (1,)), ((), ()))
STEPS = 8
TILE = 512
LANES = 128
PARTS = TILE // LANES
OUT_ROWS = 40
SIZES = (3, 3, 2)
FIRSTS = tuple(sum(SIZES[:c]) for c in range(len(SIZES)))
COLOURS = len(SIZES)
LAST = COLOURS - 1
SPLIT = 6


def mm(a, b):
    return jnp.dot(a, b, preferred_element_type=F32)


def mm_nt(a, b):
    return lax.dot_general(a, b, NT, preferred_element_type=F32)


def place_to_tile(place, brick):
    return jnp.bitwise_xor(jnp.bitwise_xor(place, jnp.right_shift(place, 2) * 2), brick)


def one_hot(local):
    low = jnp.bitwise_and(local, LANES - 1)
    rows = lax.broadcasted_iota(jnp.int16, (LANES, local.shape[1]), 0)
    match = rows == jnp.broadcast_to(low.astype(jnp.int16), rows.shape)
    return jnp.where(match, jnp.ones(rows.shape, BF16), jnp.zeros(rows.shape, BF16))


def row_of(array, step):
    return array[step : step + 1, :]


def colour_at(colour_ref, step):
    return colour_ref[0, :, step * TILE : (step + 1) * TILE].astype(F32)


def forward_kernel(
    first, brick_ref, grid_ref, samples_ref, one_ref, two_ref, three_ref, four_ref,
    partial_ref, trans_ref, hidden_ref, feature_ref, colour_ref, ray_ref, last_ref,
):
    tile = place_to_tile(pl.program_id(0) + first, brick_ref[0])
    spacing = 2.0 / (STEPS * 8)
    channels = grid_ref.shape[0]
    row = pl.program_id(0)
    for step in range(STEPS):
        span = pl.ds(step * TILE, TILE)
        local = jnp.bitwise_and(samples_ref[step : step + 1, :], TILE - 1)
        base = step * (grid_ref.shape[1] // STEPS) + tile * TILE
        pieces = [
            grid_ref[:, pl.ds(pl.multiple_of(base + k * LANES, LANES), LANES)]
            for k in range(PARTS)
        ]
        wide = mm(jnp.concatenate(pieces, axis=0), one_hot(local))
        high = jnp.broadcast_to(jnp.right_shift(local, 7), (channels, TILE))
        picked = wide[:channels]
        for k in range(1, PARTS):
            picked = jnp.where(high == k, wide[k * channels : (k + 1) * channels], picked)
        feature_ref[0, :, span] = picked.astype(BF16)
    for layer, weight_ref in enumerate((one_ref, two_ref, three_ref)):
        for step in range(STEPS):
            span = pl.ds(step * TILE, TILE)
            value = feature_ref[0, :, span] if layer == 0 else hidden_ref[0, layer - 1, :, span]
            half = mm(weight_ref[...], value)
            gate = 1.0 + jnp.tanh(half)
            hidden = half * gate
            hidden = hidden.astype(BF16)
            gate = gate.astype(BF16)
            hidden_ref[0, layer, :, span] = hidden
            hidden_ref[0, 3 + layer, :, span] = gate + hidden * (2.0 - gate)
    for step in range(STEPS):
        span = pl.ds(step * TILE, TILE)
        output = mm(four_ref[...], hidden_ref[0, 2, :, span])
        colour_ref[0, :, span] = (0.5 + 0.5 * jnp.tanh(output[:32])).astype(BF16)
        last_ref[step : step + 1, :] = output[32:33]
    half = last_ref[...]
    raw = half + half
    depth = (jnp.maximum(raw, 0.0) + jnp.log1p(jnp.exp(-jnp.abs(raw)))) * spacing
    running = [row_of(depth, 0)]
    for step in range(1, STEPS):
        running.append(running[-1] + row_of(depth, step))
    earlier = jnp.concatenate([jnp.zeros_like(running[0])] + running[:-1], axis=0)
    running = jnp.concatenate(running, axis=0)
    through = jnp.exp(-running)
    small = depth * (1.0 - depth * (0.5 - depth * (1.0 / 6.0 - depth * (1.0 / 24.0))))
    absorbed = jnp.where(depth < 0.02, small, 1.0 - jnp.exp(-depth))
    factor = jnp.exp(-earlier) * absorbed
    ray_ref[0, 0] = factor
    ray_ref[0, 1] = through
    ray_ref[0, 2] = spacing * (0.5 + 0.5 * jnp.tanh(half))
    image = row_of(factor, 0) * colour_at(colour_ref, 0)
    for step in range(1, STEPS):
        image = image + row_of(factor, step) * colour_at(colour_ref, step)
    partial_ref[0] = image
    trans_ref[pl.ds(row, 1), :] = through[STEPS - 1 : STEPS, :]


def backward_kernel(
    colour, brick_ref, samples_ref, near_ref, far_ref, weight_ref, behind_ref, hidden_ref, feature_ref,
    colour_ref, ray_ref, one_t_ref, two_t_ref, three_t_ref, four_t_ref, before_ref,
    grid_ref, packed_ref, cot_ref, out_ref, feature_cot_ref,
):
    place = pl.program_id(0) + FIRSTS[colour]
    channels = feature_ref.shape[1]

    @pl.when(pl.program_id(0) == 0)
    def _():
        if colour == 0:
            packed_ref[...] = jnp.zeros_like(packed_ref)
        else:
            packed_ref[...] = before_ref[...]

    weight = weight_ref[pl.ds(place, 1), :]
    trans_grad = weight * behind_ref[pl.ds(place, 1), :]
    factor = ray_ref[0, 0]
    through = ray_ref[0, 1]
    scaled = weight * jnp.where(place < 4, near_ref[0], far_ref[0])
    dots = jnp.concatenate(
        [
            jnp.sum(scaled * colour_at(colour_ref, step), axis=0, keepdims=True)
            for step in range(STEPS)
        ],
        axis=0,
    )
    taken = factor * dots
    later = [row_of(through, STEPS - 1) * trans_grad]
    for step in range(STEPS - 1, 0, -1):
        later.append(later[-1] + row_of(taken, step))
    depth_grad = through * dots - jnp.concatenate(later[::-1], axis=0)
    last = depth_grad * ray_ref[0, 2]
    first_row = lax.broadcasted_iota(jnp.int32, (OUT_ROWS - 32, TILE), 0) == 0
    for step in range(STEPS):
        span = pl.ds(step * TILE, TILE)
        shade = colour_at(colour_ref, step)
        out_ref[:, span] = jnp.concatenate(
            [
                (shade - shade * shade) * (row_of(factor, step) * scaled),
                jnp.where(first_row, row_of(last, step), 0.0),
            ],
            axis=0,
        ).astype(BF16)
    sums = [0.0] * 4
    for layer in (2, 1, 0):
        for step in range(STEPS):
            span = pl.ds(step * TILE, TILE)
            weight_t = (two_t_ref, three_t_ref, four_t_ref)[layer][...]
            cot = out_ref[:, span] if layer == 2 else cot_ref[layer + 1, :, span]
            cot_ref[layer, :, span] = (
                mm(weight_t, cot).astype(BF16) * hidden_ref[0, 3 + layer, :, span]
            )
            if step % 2 == 1:
                pair = pl.ds((step - 1) * TILE, 2 * TILE)
                cot = out_ref[:, pair] if layer == 2 else cot_ref[layer + 1, :, pair]
                sums[layer + 1] += mm_nt(cot, hidden_ref[0, layer, :, pair])
    for step in range(STEPS):
        span = pl.ds(step * TILE, TILE)
        feature_cot_ref[:, span] = mm(one_t_ref[...], cot_ref[0, :, span]).astype(BF16)
        if step % 2 == 1:
            pair = pl.ds((step - 1) * TILE, 2 * TILE)
            sums[0] += mm_nt(feature_ref[0, :, pair], cot_ref[0, :, pair])
    for step in range(STEPS):
        feature_cot = feature_cot_ref[:, pl.ds(step * TILE, TILE)].astype(F32)
        local = jnp.bitwise_and(samples_ref[step : step + 1, :], TILE - 1)
        high = jnp.broadcast_to(jnp.right_shift(local, 7), (channels, TILE))
        spread = jnp.concatenate(
            [jnp.where(high == k, feature_cot, 0.0) for k in range(PARTS)], axis=0
        ).astype(BF16)
        half = jnp.bitwise_xor(step // 4, brick_ref[2 + colour])
        quarter = jnp.bitwise_xor(step // 2 % 2, brick_ref[2 + COLOURS + colour])
        grid_ref[half, quarter, 0, step % 2] = mm_nt(spread, one_hot(local))

    for half in range(2):
        rows = slice(32 * half, 32 * half + 32)
        packed_ref[0, :, 128 * half : 128 * half + 64] += 0.5 * sums[1][rows]
        packed_ref[0, :, 128 * half + 64 : 128 * half + 128] += 0.5 * sums[2][rows]
    packed_ref[0, :, 256:320] += sums[3][0:32]
    packed_ref[0, 0:8, 384:448] += sums[3][32:40]
    packed_ref[0, 0:16, 320:384] += 0.5 * sums[0]


def prepare_kernel(
    grid_in_ref, samples_in_ref, one_t_in_ref, two_in_ref, three_in_ref, four_in_ref,
    grid_ref, samples_ref, one_ref, two_ref, three_ref, four_ref,
    one_t_ref, two_t_ref, three_t_ref, four_t_ref,
):
    grid_ref[...] = grid_in_ref[...]
    samples_ref[...] = samples_in_ref[...]
    one_t = one_t_in_ref[...].astype(F32) * 0.5
    one_ref[...] = one_t.T.astype(BF16)
    one_t_ref[...] = one_t.astype(BF16)
    for in_ref, plain_ref, turned_ref in (
        (two_in_ref, two_ref, two_t_ref),
        (three_in_ref, three_ref, three_t_ref),
    ):
        layer = in_ref[...].astype(F32) * 0.5
        plain_ref[...] = layer.astype(BF16)
        turned_ref[...] = layer.T.astype(BF16)
    four = four_in_ref[...].astype(F32)
    four = jnp.concatenate([four, jnp.zeros((OUT_ROWS - four.shape[0], 64), F32)], axis=0)
    four_ref[...] = (four * 0.5).astype(BF16)
    four_t_ref[...] = four.T.astype(BF16)


def flip_rows(array, flip):
    if flip == 4:
        return pltpu.roll(array, 4, 0)
    rows = lax.broadcasted_iota(jnp.int32, array.shape, 0)
    upper = jnp.bitwise_and(rows, flip) == 0
    return jnp.where(upper, pltpu.roll(array, 8 - flip, 0), pltpu.roll(array, flip, 0))


def dots_kernel(near_ref, far_ref, part_low_ref, part_high_ref, trans_low_ref, trans_high_ref, out_ref):
    out_ref[0, 0:SPLIT, :] = trans_low_ref[...]
    out_ref[0, SPLIT:8, :] = trans_high_ref[...]
    for p in range(8):
        given = near_ref[p] if p < 4 else far_ref[p - 4]
        part = part_low_ref[p] if p < SPLIT else part_high_ref[p - SPLIT]
        out_ref[1, p : p + 1, :] = jnp.sum(given * part, axis=0, keepdims=True)


def merge_kernel(level, flip, info_ref, order_ref, own_ref, got_ref, *refs):
    total, dots = own_ref[0], own_ref[1]
    got_total = flip_rows(got_ref[0], flip)
    got_dots = flip_rows(got_ref[1], flip)
    rank = jnp.bitwise_xor(info_ref[0], order_ref[0])
    bit = jnp.bitwise_and(jnp.right_shift(rank, level), 1)
    first = jnp.full(total.shape, bit, jnp.int32) == 0
    if level == 0:
        front, after, behind = jnp.ones_like(total), jnp.ones_like(total), jnp.zeros_like(total)
    else:
        state_ref, *refs = refs
        front, after, behind = state_ref[0], state_ref[1], state_ref[2]
    behind = jnp.where(first, behind + after * got_dots, behind)
    front = jnp.where(first, front, front * got_total)
    if level < 2:
        out_ref, next_ref = refs
        next_ref[0] = front
        next_ref[1] = jnp.where(first, after * got_total, after)
        next_ref[2] = behind
        out_ref[0] = total * got_total
        out_ref[1] = jnp.where(first, dots + total * got_dots, got_dots + got_total * dots)
    else:
        part_low_ref, part_high_ref, front_ref, behind_ref, image_near_ref, image_far_ref = refs
        front_ref[...] = front
        behind_ref[...] = behind
        for p in range(8):
            part = part_low_ref[p] if p < SPLIT else part_high_ref[p - SPLIT]
            image_ref = image_near_ref if p < 4 else image_far_ref
            image_ref[p % 4] = front[p : p + 1] * part


def finish_kernel(info_ref, *refs):
    sources, (packed_in_ref, grid_ref, one_t_ref, two_ref, three_ref, four_ref) = refs[: 3 * COLOURS], refs[3 * COLOURS :]
    channels = grid_ref.shape[1]
    slab = grid_ref.shape[2] // STEPS

    unit = PARTS * channels
    for colour in range(COLOURS):
        rows = 2 * SIZES[colour] * unit
        for part in range(4):
            source = sources[3 * colour + min(part, 2)]
            skip = rows if part == 3 else 0
            half = jnp.bitwise_xor(info_ref[2 + colour], part // 2)
            quarter = jnp.bitwise_xor(info_ref[2 + COLOURS + colour], part % 2)
            for at in range(SIZES[colour]):
                tile = place_to_tile(FIRSTS[colour] + at, info_ref[0])
                for step in range(2):
                    start = (half * 4 + quarter * 2 + step) * slab + tile * TILE
                    for k in range(PARTS):
                        row = skip + (at * 2 + step) * unit + k * channels
                        span = pl.ds(pl.multiple_of(start + k * LANES, LANES), LANES)
                        grid_ref[0, :, span] = source[row : row + channels, :]
    packed_in_ref = packed_in_ref[...] + sources[3 * LAST + 2][2 * rows :, :]
    one_t_ref[...] = packed_in_ref[64:80, 64:128]
    two_ref[...] = packed_in_ref[0:64, 0:64]
    three_ref[...] = packed_in_ref[0:64, 64:128]
    four_ref[...] = packed_in_ref[64:97, 0:64]


VMEM = pl.BlockSpec(memory_space=pltpu.VMEM)
SMEM = pl.BlockSpec(memory_space=pltpu.SMEM)
SMALL = pltpu.CompilerParams(vmem_limit_bytes=4 * 2**20)


def run_prepare(grid, samples, one_t, two, three, four):
    channels = one_t.shape[0]
    shapes = [(64, channels), (64, 64), (64, 64), (OUT_ROWS, 64)]
    shapes += [shape[::-1] for shape in shapes]
    return pl.pallas_call(
        prepare_kernel,
        out_shape=[
            jax.ShapeDtypeStruct(grid.shape, grid.dtype),
            jax.ShapeDtypeStruct(samples.shape, samples.dtype),
            *[jax.ShapeDtypeStruct(shape, BF16) for shape in shapes],
        ],
        in_specs=[VMEM] * 6,
        out_specs=[VMEM] * 10,
        compiler_params=SMALL,
        name="prepare",
    )(grid, samples, one_t, two, three, four)


def run_dots(*arrays):
    return pl.pallas_call(
        dots_kernel,
        out_shape=jax.ShapeDtypeStruct((2, 8, TILE), F32),
        in_specs=[VMEM] * 6,
        out_specs=VMEM,
        compiler_params=SMALL,
        name="dots",
    )(*arrays)


def run_merge(level, flip, info, order, own, got, *more):
    shapes = {
        False: [(2, 8, TILE), (3, 8, TILE)],
        True: [(8, TILE), (8, TILE), (4, 32, TILE), (4, 32, TILE)],
    }[level == 2]
    return pl.pallas_call(
        functools.partial(merge_kernel, level, flip),
        out_shape=[jax.ShapeDtypeStruct(shape, F32) for shape in shapes],
        in_specs=[SMEM, SMEM] + [VMEM] * (2 + len(more)),
        out_specs=[VMEM] * len(shapes),
        compiler_params=SMALL,
        name="merge",
    )(info, order, own, got, *more)


def whole(shape):
    return pl.BlockSpec(shape, lambda p, brick: (0,) * len(shape))


def at_place(shape):
    return pl.BlockSpec((1,) + shape, lambda p, brick: (p,) + (0,) * len(shape))


def run_forward(first, count, brick, grid, samples, one, two, three, four):
    wide = STEPS * TILE
    channels = grid.shape[0]
    shapes = [
        jax.ShapeDtypeStruct((count, 32, TILE), F32),
        jax.ShapeDtypeStruct((count, TILE), F32),
        jax.ShapeDtypeStruct((count, 6, 64, wide), BF16),
        jax.ShapeDtypeStruct((count, channels, wide), BF16),
        jax.ShapeDtypeStruct((count, 32, wide), BF16),
        jax.ShapeDtypeStruct((count, 3, STEPS, TILE), F32),
    ]
    return pl.pallas_call(
        functools.partial(forward_kernel, first),
        out_shape=shapes,
        grid_spec=pltpu.PrefetchScalarGridSpec(
            num_scalar_prefetch=1,
            grid=(count,),
            in_specs=[
                whole(grid.shape),
                pl.BlockSpec(
                    (STEPS, TILE), lambda p, brick: (0, place_to_tile(p + first, brick[0]))
                ),
                whole(one.shape),
                whole(two.shape),
                whole(three.shape),
                whole(four.shape),
            ],
            out_specs=[
                at_place((32, TILE)),
                whole((count, TILE)),
                at_place((6, 64, wide)),
                at_place((channels, wide)),
                at_place((32, wide)),
                at_place((3, STEPS, TILE)),
            ],
            scratch_shapes=[pltpu.VMEM((STEPS, TILE), F32)],
        ),
        cost_estimate=pl.CostEstimate(
            flops=250_000_000 * count,
            bytes_accessed=4_000_000 * count,
            transcendentals=1_000_000 * count,
        ),
        compiler_params=pltpu.CompilerParams(vmem_limit_bytes=14 * 2**20),
        name="forward",
    )(brick, grid, samples, one, two, three, four)


def run_backward(colour, brick, samples, near, far, weight, behind, saved, layers, before):
    count = SIZES[colour]
    first = FIRSTS[colour]
    skip = first % SPLIT
    wide = STEPS * TILE
    hidden, feature, shade, ray = saved
    channels = feature.shape[1]

    def later(shape):
        return pl.BlockSpec((1,) + shape, lambda p, brick: (p + skip,) + (0,) * len(shape))

    return pl.pallas_call(
        functools.partial(backward_kernel, colour),
        out_shape=[
            jax.ShapeDtypeStruct((2, 2, count, 2, PARTS * channels, LANES), F32),
            jax.ShapeDtypeStruct((1, 32, TILE), F32),
        ],
        grid_spec=pltpu.PrefetchScalarGridSpec(
            num_scalar_prefetch=1,
            grid=(count,),
            in_specs=[
                pl.BlockSpec(
                    (STEPS, TILE), lambda p, brick: (0, place_to_tile(p + first, brick[0]))
                ),
                pl.BlockSpec((1, 32, TILE), lambda p, brick: (jnp.minimum(p + first, 3), 0, 0)),
                pl.BlockSpec((1, 32, TILE), lambda p, brick: (jnp.maximum(p + first, 4) - 4, 0, 0)),
                whole(weight.shape),
                whole(behind.shape),
                later((6, 64, wide)),
                later((channels, wide)),
                later((32, wide)),
                later((3, STEPS, TILE)),
                *[whole(layer.shape) for layer in layers],
                whole((1, 32, TILE)),
            ],
            out_specs=[
                pl.BlockSpec(
                    (2, 2, 1, 2, PARTS * channels, LANES), lambda p, brick: (0, 0, p, 0, 0, 0)
                ),
                whole((1, 32, TILE)),
            ],
            scratch_shapes=[
                pltpu.VMEM((3, 64, wide), BF16),
                pltpu.VMEM((OUT_ROWS, wide), BF16),
                pltpu.VMEM((channels, wide), BF16),
            ],
        ),
        cost_estimate=pl.CostEstimate(
            flops=500_000_000 * count, bytes_accessed=4_500_000 * count, transcendentals=0
        ),
        compiler_params=pltpu.CompilerParams(vmem_limit_bytes=14 * 2**20),
        name="backward",
    )(
        brick, samples, near, far, weight, behind, hidden, feature, shade, ray, *layers, before
    )


def run_finish(info, sources, packed, channels, voxels):
    return pl.pallas_call(
        finish_kernel,
        out_shape=[
            jax.ShapeDtypeStruct((1, channels, voxels), F32),
            jax.ShapeDtypeStruct((channels, 64), F32),
            jax.ShapeDtypeStruct((64, 64), F32),
            jax.ShapeDtypeStruct((64, 64), F32),
            jax.ShapeDtypeStruct((33, 64), F32),
        ],
        in_specs=[SMEM] + [VMEM] * (3 * COLOURS + 1),
        out_specs=[VMEM] * 5,
        compiler_params=pltpu.CompilerParams(vmem_limit_bytes=14 * 2**20),
        name="finish",
    )(info, *sources, packed)


def swap_brick(array, flip):
    return lax.ppermute(array, "brick", [(i, i ^ flip) for i in range(8)])


def link_of(colour, turn, odd):
    return (2 * colour + turn + 2 * odd) % 4


def view_swap(array, colour, turn):
    pairs = []
    for view in range(16):
        y, x = view // 4, view % 4
        for brick in range(8):
            dim = link_of(colour, turn, brick % 2)
            flip = 1 if dim < 2 else 3
            other = y * 4 + (x ^ flip) if dim % 2 == 0 else (y ^ flip) * 4 + x
            pairs.append((brick * 16 + view, brick * 16 + other))
    return lax.ppermute(array, ("brick", "view"), pairs)


def make_info(brick):
    view = lax.axis_index("view")
    y = jnp.right_shift(view, 2)
    x = jnp.bitwise_and(view, 3)
    bits = [
        jnp.bitwise_and(x ^ (x >> 1), 1),
        jnp.bitwise_and(y ^ (y >> 1), 1),
        x >> 1,
        y >> 1,
    ]
    odd = jnp.bitwise_and(brick, 1) == 1
    values = [brick, brick]
    for turn in range(2):
        for colour in range(COLOURS):
            even_bit, odd_bit = (bits[link_of(colour, turn, at)] for at in range(2))
            values.append(jnp.where(odd, odd_bit, even_bit))
    return jnp.stack(values).astype(jnp.int32)


def work(
    latent_grid, layer_one, layer_two, layer_three, layer_four, view_order, samples, pixel_grad
):
    brick = lax.axis_index("brick")
    info = make_info(brick)
    voxels = latent_grid.shape[2]

    latent, index, *layers = run_prepare(
        *[
            pltpu.with_memory_space_constraint(array, pltpu.HBM)
            for array in (
                latent_grid[0], samples[0, 0], layer_one.T, layer_two, layer_three, layer_four,
            )
        ]
    )
    plain, turned = layers[:4], layers[4:]

    near = [pixel_grad] + [swap_brick(pixel_grad, flip) for flip in (1, 2, 3)]
    part_low, trans_low, *saved_low = run_forward(0, SPLIT, info, latent, index, *plain)
    near = jnp.concatenate(near, axis=0)
    far = swap_brick(near, 6)
    part_high, trans_high, *saved_high = run_forward(SPLIT, 8 - SPLIT, info, latent, index, *plain)

    own = run_dots(near, far, part_low, part_high, trans_low, trans_high)
    own, state = run_merge(0, 1, info, view_order, own, swap_brick(own, 1))
    own, state = run_merge(1, 2, info, view_order, own, swap_brick(own, 2), state)
    front, behind, image_near, image_far = run_merge(
        2, 4, info, view_order, own, swap_brick(own, 6), state, part_low, part_high
    )

    image = image_near + swap_brick(image_far, 6)
    image = image[:2] + swap_brick(image[2:], 2)
    image = image[:1] + swap_brick(image[1:], 1)

    packed = jnp.zeros((1, 32, TILE), F32)
    grids = []
    for colour in range(COLOURS):
        saved = saved_low if FIRSTS[colour] < SPLIT else saved_high
        grid, packed = run_backward(
            colour, info, index, near, far, front, behind, saved, turned, packed
        )
        grids.append(grid)
    for flip in (1, 2, 6):
        packed = packed + swap_brick(packed, flip)
    packed = jnp.concatenate([packed[0, :, k * LANES : (k + 1) * LANES] for k in range(4)], axis=0)
    packed = packed[:104]

    sources = []
    for colour in range(COLOURS):
        part = grids[colour]
        for turn in range(2):
            part = part[0] + view_swap(part[1], colour, turn)
        part = part.reshape(-1, LANES)
        rows = part.shape[0]
        if colour == LAST:
            part = jnp.concatenate([part, packed], axis=0)
        for turn in (2, 3):
            part = part + view_swap(part, colour, turn)
        got = view_swap(part, colour, 1)
        sent = jnp.concatenate([part[:rows], got[:rows]], axis=0)
        if colour == LAST:
            packed = part[rows:] + got[rows:]
            sent = jnp.concatenate([sent, packed], axis=0)
        sources += [part, got, view_swap(sent, colour, 0)]

    channels = latent_grid.shape[1]
    grid, one_t, two, three, four = run_finish(info, sources, packed, channels, voxels)
    return (image, grid, one_t.T, two, three, four)


def solution(mesh):
    in_specs = (
        P("brick", None, None),
        P(),
        P(),
        P(),
        P(),
        P("view"),
        P("view", "brick", None, None),
        P("view", None, "brick"),
    )
    out_specs = (P("view", None, "brick"), P("brick", None, None), P(), P(), P(), P())
    return jax.shard_map(work, mesh=mesh, in_specs=in_specs, out_specs=out_specs, check_vma=False)
```

```python
import functools

import jax
import jax.numpy as jnp
from jax import lax
from jax.experimental import pallas as pl
from jax.experimental.pallas import tpu as pltpu
from jax.sharding import PartitionSpec as P


F32 = jnp.float32
BF16 = jnp.bfloat16
NT = (((1,), (1,)), ((), ()))
STEPS = 8
TILE = 512
LANES = 128
PARTS = TILE // LANES
OUT_ROWS = 40
SIZES = (3, 3, 2)
FIRSTS = tuple(sum(SIZES[:c]) for c in range(len(SIZES)))
COLOURS = len(SIZES)
LAST = COLOURS - 1
SPLIT = 3


def mm(a, b):
    return jnp.dot(a, b, preferred_element_type=F32)


def mm_nt(a, b):
    return lax.dot_general(a, b, NT, preferred_element_type=F32)


def place_to_tile(place, brick):
    return jnp.bitwise_xor(jnp.bitwise_xor(place, jnp.right_shift(place, 2) * 2), brick)


def one_hot(local):
    low = jnp.bitwise_and(local, LANES - 1)
    rows = lax.broadcasted_iota(jnp.int16, (LANES, local.shape[1]), 0)
    match = rows == jnp.broadcast_to(low.astype(jnp.int16), rows.shape)
    return jnp.where(match, jnp.ones(rows.shape, BF16), jnp.zeros(rows.shape, BF16))


def row_of(array, step):
    return array[step : step + 1, :]


def colour_at(colour_ref, step):
    return colour_ref[0, :, step * TILE : (step + 1) * TILE].astype(F32)


def forward_kernel(
    first, brick_ref, grid_ref, samples_ref, one_ref, two_ref, three_ref, four_ref,
    partial_ref, trans_ref, hidden_ref, feature_ref, colour_ref, ray_ref, last_ref,
):
    tile = place_to_tile(pl.program_id(0) + first, brick_ref[0])
    spacing = 2.0 / (STEPS * 8)
    channels = grid_ref.shape[0]
    row = pl.program_id(0)
    for step in range(STEPS):
        span = pl.ds(step * TILE, TILE)
        local = jnp.bitwise_and(samples_ref[step : step + 1, :], TILE - 1)
        base = step * (grid_ref.shape[1] // STEPS) + tile * TILE
        pieces = [
            grid_ref[:, pl.ds(pl.multiple_of(base + k * LANES, LANES), LANES)]
            for k in range(PARTS)
        ]
        wide = mm(jnp.concatenate(pieces, axis=0), one_hot(local))
        high = jnp.broadcast_to(jnp.right_shift(local, 7), (channels, TILE))
        picked = wide[:channels]
        for k in range(1, PARTS):
            picked = jnp.where(high == k, wide[k * channels : (k + 1) * channels], picked)
        feature_ref[0, :, span] = picked.astype(BF16)
    for layer, weight_ref in enumerate((one_ref, two_ref, three_ref)):
        for step in range(STEPS):
            span = pl.ds(step * TILE, TILE)
            value = feature_ref[0, :, span] if layer == 0 else hidden_ref[0, layer - 1, :, span]
            half = mm(weight_ref[...], value)
            gate = 1.0 + jnp.tanh(half)
            hidden = half * gate
            hidden = hidden.astype(BF16)
            gate = gate.astype(BF16)
            hidden_ref[0, layer, :, span] = hidden
            hidden_ref[0, 3 + layer, :, span] = gate + hidden * (2.0 - gate)
    for step in range(STEPS):
        span = pl.ds(step * TILE, TILE)
        output = mm(four_ref[...], hidden_ref[0, 2, :, span])
        colour_ref[0, :, span] = (0.5 + 0.5 * jnp.tanh(output[:32])).astype(BF16)
        last_ref[step : step + 1, :] = output[32:33]
    half = last_ref[...]
    raw = half + half
    depth = (jnp.maximum(raw, 0.0) + jnp.log1p(jnp.exp(-jnp.abs(raw)))) * spacing
    running = [row_of(depth, 0)]
    for step in range(1, STEPS):
        running.append(running[-1] + row_of(depth, step))
    earlier = jnp.concatenate([jnp.zeros_like(running[0])] + running[:-1], axis=0)
    running = jnp.concatenate(running, axis=0)
    through = jnp.exp(-running)
    small = depth * (1.0 - depth * (0.5 - depth * (1.0 / 6.0 - depth * (1.0 / 24.0))))
    absorbed = jnp.where(depth < 0.02, small, 1.0 - jnp.exp(-depth))
    factor = jnp.exp(-earlier) * absorbed
    ray_ref[0, 0] = factor
    ray_ref[0, 1] = through
    ray_ref[0, 2] = spacing * (0.5 + 0.5 * jnp.tanh(half))
    image = row_of(factor, 0) * colour_at(colour_ref, 0)
    for step in range(1, STEPS):
        image = image + row_of(factor, step) * colour_at(colour_ref, step)
    partial_ref[0] = image
    trans_ref[pl.ds(row, 1), :] = through[STEPS - 1 : STEPS, :]


def backward_kernel(
    colour, brick_ref, samples_ref, near_ref, far_ref, weight_ref, behind_ref, hidden_ref, feature_ref,
    colour_ref, ray_ref, one_t_ref, two_t_ref, three_t_ref, four_t_ref, before_ref,
    grid_ref, packed_ref, cot_ref, out_ref, feature_cot_ref,
):
    place = pl.program_id(0) + FIRSTS[colour]
    channels = feature_ref.shape[1]

    @pl.when(pl.program_id(0) == 0)
    def _():
        if colour == 0:
            packed_ref[...] = jnp.zeros_like(packed_ref)
        else:
            packed_ref[...] = before_ref[...]

    weight = weight_ref[pl.ds(place, 1), :]
    trans_grad = weight * behind_ref[pl.ds(place, 1), :]
    factor = ray_ref[0, 0]
    through = ray_ref[0, 1]
    scaled = weight * jnp.where(place < 4, near_ref[0], far_ref[0])
    dots = jnp.concatenate(
        [
            jnp.sum(scaled * colour_at(colour_ref, step), axis=0, keepdims=True)
            for step in range(STEPS)
        ],
        axis=0,
    )
    taken = factor * dots
    later = [row_of(through, STEPS - 1) * trans_grad]
    for step in range(STEPS - 1, 0, -1):
        later.append(later[-1] + row_of(taken, step))
    depth_grad = through * dots - jnp.concatenate(later[::-1], axis=0)
    last = depth_grad * ray_ref[0, 2]
    first_row = lax.broadcasted_iota(jnp.int32, (OUT_ROWS - 32, TILE), 0) == 0
    for step in range(STEPS):
        span = pl.ds(step * TILE, TILE)
        shade = colour_at(colour_ref, step)
        out_ref[:, span] = jnp.concatenate(
            [
                (shade - shade * shade) * (row_of(factor, step) * scaled),
                jnp.where(first_row, row_of(last, step), 0.0),
            ],
            axis=0,
        ).astype(BF16)
    sums = [0.0] * 4
    for layer in (2, 1, 0):
        for step in range(STEPS):
            span = pl.ds(step * TILE, TILE)
            weight_t = (two_t_ref, three_t_ref, four_t_ref)[layer][...]
            cot = out_ref[:, span] if layer == 2 else cot_ref[layer + 1, :, span]
            cot_ref[layer, :, span] = (
                mm(weight_t, cot).astype(BF16) * hidden_ref[0, 3 + layer, :, span]
            )
            if step % 2 == 1:
                pair = pl.ds((step - 1) * TILE, 2 * TILE)
                cot = out_ref[:, pair] if layer == 2 else cot_ref[layer + 1, :, pair]
                sums[layer + 1] += mm_nt(cot, hidden_ref[0, layer, :, pair])
    for step in range(STEPS):
        span = pl.ds(step * TILE, TILE)
        feature_cot_ref[:, span] = mm(one_t_ref[...], cot_ref[0, :, span]).astype(BF16)
        if step % 2 == 1:
            pair = pl.ds((step - 1) * TILE, 2 * TILE)
            sums[0] += mm_nt(feature_ref[0, :, pair], cot_ref[0, :, pair])
    for step in range(STEPS):
        feature_cot = feature_cot_ref[:, pl.ds(step * TILE, TILE)].astype(F32)
        local = jnp.bitwise_and(samples_ref[step : step + 1, :], TILE - 1)
        high = jnp.broadcast_to(jnp.right_shift(local, 7), (channels, TILE))
        spread = jnp.concatenate(
            [jnp.where(high == k, feature_cot, 0.0) for k in range(PARTS)], axis=0
        ).astype(BF16)
        half = jnp.bitwise_xor(step // 4, brick_ref[2 + colour])
        quarter = jnp.bitwise_xor(step // 2 % 2, brick_ref[2 + COLOURS + colour])
        grid_ref[half, quarter, 0, step % 2] = mm_nt(spread, one_hot(local))

    for half in range(2):
        rows = slice(32 * half, 32 * half + 32)
        packed_ref[0, :, 128 * half : 128 * half + 64] += 0.5 * sums[1][rows]
        packed_ref[0, :, 128 * half + 64 : 128 * half + 128] += 0.5 * sums[2][rows]
    packed_ref[0, :, 256:320] += sums[3][0:32]
    packed_ref[0, 0:8, 384:448] += sums[3][32:40]
    packed_ref[0, 0:16, 320:384] += 0.5 * sums[0]


def prepare_kernel(
    grid_in_ref, samples_in_ref, given_in_ref, one_t_in_ref, two_in_ref, three_in_ref, four_in_ref,
    grid_ref, samples_ref, given_ref, one_ref, two_ref, three_ref, four_ref,
    one_t_ref, two_t_ref, three_t_ref, four_t_ref,
):
    grid_ref[...] = grid_in_ref[...]
    samples_ref[...] = samples_in_ref[...]
    given_ref[...] = given_in_ref[...]
    one_t = one_t_in_ref[...].astype(F32) * 0.5
    one_ref[...] = one_t.T.astype(BF16)
    one_t_ref[...] = one_t.astype(BF16)
    for in_ref, plain_ref, turned_ref in (
        (two_in_ref, two_ref, two_t_ref),
        (three_in_ref, three_ref, three_t_ref),
    ):
        layer = in_ref[...].astype(F32) * 0.5
        plain_ref[...] = layer.astype(BF16)
        turned_ref[...] = layer.T.astype(BF16)
    four = four_in_ref[...].astype(F32)
    four = jnp.concatenate([four, jnp.zeros((OUT_ROWS - four.shape[0], 64), F32)], axis=0)
    four_ref[...] = (four * 0.5).astype(BF16)
    four_t_ref[...] = four.T.astype(BF16)


def flip_rows(array, flip):
    if flip == 4:
        return pltpu.roll(array, 4, 0)
    rows = lax.broadcasted_iota(jnp.int32, array.shape, 0)
    upper = jnp.bitwise_and(rows, flip) == 0
    return jnp.where(upper, pltpu.roll(array, 8 - flip, 0), pltpu.roll(array, flip, 0))


def dots_kernel(near_ref, far_ref, part_low_ref, part_high_ref, trans_low_ref, trans_high_ref, out_ref):
    out_ref[0, 0:SPLIT, :] = trans_low_ref[...]
    out_ref[0, SPLIT:8, :] = trans_high_ref[...]
    for p in range(8):
        given = near_ref[p] if p < 4 else far_ref[p - 4]
        part = part_low_ref[p] if p < SPLIT else part_high_ref[p - SPLIT]
        out_ref[1, p : p + 1, :] = jnp.sum(given * part, axis=0, keepdims=True)


def first_of(rank, level, shape):
    bit = jnp.bitwise_and(jnp.right_shift(rank, level), 1)
    return jnp.full(shape, bit, jnp.int32) == 0


def joined(first, total, dots, other_total, other_dots):
    return total * other_total, jnp.where(
        first, dots + total * other_dots, other_dots + other_total * dots
    )


def quad_kernel(info_ref, order_ref, own_ref, one_ref, two_ref, three_ref, out_ref, next_ref):
    total, dots = own_ref[0], own_ref[1]
    rank = jnp.bitwise_xor(info_ref[0], order_ref[0])
    ones, zeros = jnp.ones_like(total), jnp.zeros_like(total)
    first = first_of(rank, 0, total.shape)
    one_total, one_dots = (flip_rows(one_ref[i], 1) for i in range(2))
    two_total, two_dots = (flip_rows(two_ref[i], 2) for i in range(2))
    three_total, three_dots = (flip_rows(flip_rows(three_ref[i], 1), 2) for i in range(2))
    behind = jnp.where(first, one_dots, zeros)
    after = jnp.where(first, one_total, ones)
    front = jnp.where(first, ones, one_total)
    total, dots = joined(first, total, dots, one_total, one_dots)
    other_total, other_dots = joined(first, two_total, two_dots, three_total, three_dots)
    first = first_of(rank, 1, total.shape)
    next_ref[0] = jnp.where(first, front, front * other_total)
    next_ref[1] = jnp.where(first, behind + after * other_dots, behind)
    next_ref[2] = jnp.where(first, after * other_total, after)
    out_ref[0], out_ref[1] = joined(first, total, dots, other_total, other_dots)


def eight_kernel(
    info_ref, order_ref, got_ref, state_ref, part_low_ref, part_high_ref,
    front_ref, behind_ref, image_near_ref, image_far_ref,
):
    got_total, got_dots = flip_rows(got_ref[0], 4), flip_rows(got_ref[1], 4)
    rank = jnp.bitwise_xor(info_ref[0], order_ref[0])
    first = first_of(rank, 2, got_total.shape)
    front = jnp.where(first, state_ref[0], state_ref[0] * got_total)
    front_ref[...] = front
    behind_ref[...] = jnp.where(first, state_ref[1] + state_ref[2] * got_dots, state_ref[1])
    for p in range(8):
        part = part_low_ref[p] if p < SPLIT else part_high_ref[p - SPLIT]
        image_ref = image_near_ref if p < 4 else image_far_ref
        image_ref[p % 4] = front[p : p + 1] * part


def finish_kernel(info_ref, *refs):
    sources, (packed_in_ref, grid_ref, one_t_ref, two_ref, three_ref, four_ref) = refs[: 3 * COLOURS], refs[3 * COLOURS :]
    channels = grid_ref.shape[1]
    slab = grid_ref.shape[2] // STEPS

    unit = PARTS * channels
    for colour in range(COLOURS):
        rows = 2 * SIZES[colour] * unit
        for part in range(4):
            source = sources[3 * colour + min(part, 2)]
            skip = rows if part == 3 else 0
            half = jnp.bitwise_xor(info_ref[2 + colour], part // 2)
            quarter = jnp.bitwise_xor(info_ref[2 + COLOURS + colour], part % 2)
            for at in range(SIZES[colour]):
                tile = place_to_tile(FIRSTS[colour] + at, info_ref[0])
                for step in range(2):
                    start = (half * 4 + quarter * 2 + step) * slab + tile * TILE
                    for k in range(PARTS):
                        row = skip + (at * 2 + step) * unit + k * channels
                        span = pl.ds(pl.multiple_of(start + k * LANES, LANES), LANES)
                        grid_ref[0, :, span] = source[row : row + channels, :]
    packed_in_ref = packed_in_ref[...] + sources[3 * LAST + 2][2 * rows :, :]
    one_t_ref[...] = packed_in_ref[64:80, 64:128]
    two_ref[...] = packed_in_ref[0:64, 0:64]
    three_ref[...] = packed_in_ref[0:64, 64:128]
    four_ref[...] = packed_in_ref[64:97, 0:64]


VMEM = pl.BlockSpec(memory_space=pltpu.VMEM)
SMEM = pl.BlockSpec(memory_space=pltpu.SMEM)
SMALL = pltpu.CompilerParams(vmem_limit_bytes=4 * 2**20)


def run_prepare(grid, samples, given, one_t, two, three, four):
    channels = one_t.shape[0]
    shapes = [(64, channels), (64, 64), (64, 64), (OUT_ROWS, 64)]
    shapes += [shape[::-1] for shape in shapes]
    return pl.pallas_call(
        prepare_kernel,
        out_shape=[
            jax.ShapeDtypeStruct(grid.shape, grid.dtype),
            jax.ShapeDtypeStruct(samples.shape, samples.dtype),
            jax.ShapeDtypeStruct(given.shape, given.dtype),
            *[jax.ShapeDtypeStruct(shape, BF16) for shape in shapes],
        ],
        in_specs=[VMEM] * 7,
        out_specs=[VMEM] * 11,
        compiler_params=SMALL,
        name="prepare",
    )(grid, samples, given, one_t, two, three, four)


def run_dots(*arrays):
    return pl.pallas_call(
        dots_kernel,
        out_shape=jax.ShapeDtypeStruct((2, 8, TILE), F32),
        in_specs=[VMEM] * 6,
        out_specs=VMEM,
        compiler_params=SMALL,
        name="dots",
    )(*arrays)


def run_quad(info, order, *arrays):
    return pl.pallas_call(
        quad_kernel,
        out_shape=[jax.ShapeDtypeStruct((n, 8, TILE), F32) for n in (2, 3)],
        in_specs=[SMEM, SMEM] + [VMEM] * 4,
        out_specs=[VMEM] * 2,
        compiler_params=SMALL,
        name="quad",
    )(info, order, *arrays)


def run_eight(info, order, *arrays):
    shapes = [(8, TILE), (8, TILE), (4, 32, TILE), (4, 32, TILE)]
    return pl.pallas_call(
        eight_kernel,
        out_shape=[jax.ShapeDtypeStruct(shape, F32) for shape in shapes],
        in_specs=[SMEM, SMEM] + [VMEM] * 4,
        out_specs=[VMEM] * 4,
        compiler_params=SMALL,
        name="eight",
    )(info, order, *arrays)


def whole(shape):
    return pl.BlockSpec(shape, lambda p, brick: (0,) * len(shape))


def at_place(shape):
    return pl.BlockSpec((1,) + shape, lambda p, brick: (p,) + (0,) * len(shape))


def run_forward(first, count, brick, grid, samples, one, two, three, four):
    wide = STEPS * TILE
    channels = grid.shape[0]
    shapes = [
        jax.ShapeDtypeStruct((count, 32, TILE), F32),
        jax.ShapeDtypeStruct((count, TILE), F32),
        jax.ShapeDtypeStruct((count, 6, 64, wide), BF16),
        jax.ShapeDtypeStruct((count, channels, wide), BF16),
        jax.ShapeDtypeStruct((count, 32, wide), BF16),
        jax.ShapeDtypeStruct((count, 3, STEPS, TILE), F32),
    ]
    return pl.pallas_call(
        functools.partial(forward_kernel, first),
        out_shape=shapes,
        grid_spec=pltpu.PrefetchScalarGridSpec(
            num_scalar_prefetch=1,
            grid=(count,),
            in_specs=[
                whole(grid.shape),
                pl.BlockSpec(
                    (STEPS, TILE), lambda p, brick: (0, place_to_tile(p + first, brick[0]))
                ),
                whole(one.shape),
                whole(two.shape),
                whole(three.shape),
                whole(four.shape),
            ],
            out_specs=[
                at_place((32, TILE)),
                whole((count, TILE)),
                at_place((6, 64, wide)),
                at_place((channels, wide)),
                at_place((32, wide)),
                at_place((3, STEPS, TILE)),
            ],
            scratch_shapes=[pltpu.VMEM((STEPS, TILE), F32)],
        ),
        cost_estimate=pl.CostEstimate(
            flops=250_000_000 * count,
            bytes_accessed=4_000_000 * count,
            transcendentals=1_000_000 * count,
        ),
        compiler_params=pltpu.CompilerParams(vmem_limit_bytes=14 * 2**20),
        name="forward",
    )(brick, grid, samples, one, two, three, four)


def run_backward(colour, brick, samples, near, far, weight, behind, saved, layers, before):
    count = SIZES[colour]
    first = FIRSTS[colour]
    skip = first if first < SPLIT else first - SPLIT
    wide = STEPS * TILE
    hidden, feature, shade, ray = saved
    channels = feature.shape[1]

    def later(shape):
        return pl.BlockSpec((1,) + shape, lambda p, brick: (p + skip,) + (0,) * len(shape))

    return pl.pallas_call(
        functools.partial(backward_kernel, colour),
        out_shape=[
            jax.ShapeDtypeStruct((2, 2, count, 2, PARTS * channels, LANES), F32),
            jax.ShapeDtypeStruct((1, 32, TILE), F32),
        ],
        grid_spec=pltpu.PrefetchScalarGridSpec(
            num_scalar_prefetch=1,
            grid=(count,),
            in_specs=[
                pl.BlockSpec(
                    (STEPS, TILE), lambda p, brick: (0, place_to_tile(p + first, brick[0]))
                ),
                pl.BlockSpec((1, 32, TILE), lambda p, brick: (jnp.minimum(p + first, 3), 0, 0)),
                pl.BlockSpec((1, 32, TILE), lambda p, brick: (jnp.maximum(p + first, 4) - 4, 0, 0)),
                whole(weight.shape),
                whole(behind.shape),
                later((6, 64, wide)),
                later((channels, wide)),
                later((32, wide)),
                later((3, STEPS, TILE)),
                *[whole(layer.shape) for layer in layers],
                whole((1, 32, TILE)),
            ],
            out_specs=[
                pl.BlockSpec(
                    (2, 2, 1, 2, PARTS * channels, LANES), lambda p, brick: (0, 0, p, 0, 0, 0)
                ),
                whole((1, 32, TILE)),
            ],
            scratch_shapes=[
                pltpu.VMEM((3, 64, wide), BF16),
                pltpu.VMEM((OUT_ROWS, wide), BF16),
                pltpu.VMEM((channels, wide), BF16),
            ],
        ),
        cost_estimate=pl.CostEstimate(
            flops=500_000_000 * count, bytes_accessed=4_500_000 * count, transcendentals=0
        ),
        compiler_params=pltpu.CompilerParams(vmem_limit_bytes=14 * 2**20),
        name="backward",
    )(
        brick, samples, near, far, weight, behind, hidden, feature, shade, ray, *layers, before
    )


def run_finish(info, sources, packed, channels, voxels):
    return pl.pallas_call(
        finish_kernel,
        out_shape=[
            jax.ShapeDtypeStruct((1, channels, voxels), F32),
            jax.ShapeDtypeStruct((channels, 64), F32),
            jax.ShapeDtypeStruct((64, 64), F32),
            jax.ShapeDtypeStruct((64, 64), F32),
            jax.ShapeDtypeStruct((33, 64), F32),
        ],
        in_specs=[SMEM] + [VMEM] * (3 * COLOURS + 1),
        out_specs=[VMEM] * 5,
        compiler_params=pltpu.CompilerParams(vmem_limit_bytes=14 * 2**20),
        name="finish",
    )(info, *sources, packed)


def swap_brick(array, flip):
    return lax.ppermute(array, "brick", [(i, i ^ flip) for i in range(8)])


def link_of(colour, turn, odd):
    return (2 * colour + turn + 2 * odd) % 4


def view_swap(array, colour, turn):
    pairs = []
    for view in range(16):
        y, x = view // 4, view % 4
        for brick in range(8):
            dim = link_of(colour, turn, brick % 2)
            flip = 1 if dim < 2 else 3
            other = y * 4 + (x ^ flip) if dim % 2 == 0 else (y ^ flip) * 4 + x
            pairs.append((brick * 16 + view, brick * 16 + other))
    return lax.ppermute(array, ("brick", "view"), pairs)


def make_info(brick):
    view = lax.axis_index("view")
    y = jnp.right_shift(view, 2)
    x = jnp.bitwise_and(view, 3)
    bits = [
        jnp.bitwise_and(x ^ (x >> 1), 1),
        jnp.bitwise_and(y ^ (y >> 1), 1),
        x >> 1,
        y >> 1,
    ]
    odd = jnp.bitwise_and(brick, 1) == 1
    values = [brick, brick]
    for turn in range(2):
        for colour in range(COLOURS):
            even_bit, odd_bit = (bits[link_of(colour, turn, at)] for at in range(2))
            values.append(jnp.where(odd, odd_bit, even_bit))
    return jnp.stack(values).astype(jnp.int32)


def work(
    latent_grid, layer_one, layer_two, layer_three, layer_four, view_order, samples, pixel_grad
):
    brick = lax.axis_index("brick")
    info = make_info(brick)
    voxels = latent_grid.shape[2]

    latent, index, given, *layers = run_prepare(
        *[
            pltpu.with_memory_space_constraint(array, pltpu.HBM)
            for array in (
                latent_grid[0], samples[0, 0], pixel_grad, layer_one.T, layer_two, layer_three, layer_four,
            )
        ]
    )
    plain, turned = layers[:4], layers[4:]

    near = [given] + [swap_brick(pixel_grad, flip) for flip in (1, 2, 3)]
    part_low, trans_low, *saved_low = run_forward(0, SPLIT, info, latent, index, *plain)
    near = jnp.concatenate(near, axis=0)
    far = swap_brick(near, 6)
    part_high, trans_high, *saved_high = run_forward(SPLIT, 8 - SPLIT, info, latent, index, *plain)

    own = run_dots(near, far, part_low, part_high, trans_low, trans_high)
    got = [swap_brick(own, flip) for flip in (2, 3, 1)]
    own, state = run_quad(info, view_order, own, got[2], got[0], got[1])
    front, behind, image_near, image_far = run_eight(
        info, view_order, swap_brick(own, 6), state, part_low, part_high
    )

    image = image_near + swap_brick(image_far, 6)
    image = image[:2] + swap_brick(image[2:], 2)
    image = image[:1] + swap_brick(image[1:], 1)

    packed = jnp.zeros((1, 32, TILE), F32)
    grids = []
    for colour in range(COLOURS):
        saved = saved_low if FIRSTS[colour] < SPLIT else saved_high
        grid, packed = run_backward(
            colour, info, index, near, far, front, behind, saved, turned, packed
        )
        grids.append(grid)
    got = [swap_brick(packed, flip) for flip in (1, 2, 3)]
    packed = packed + got[0] + (got[1] + got[2])
    packed = packed + swap_brick(packed, 6)
    packed = jnp.concatenate([packed[0, :, k * LANES : (k + 1) * LANES] for k in range(4)], axis=0)
    packed = packed[:104]

    sources = []
    for colour in range(COLOURS):
        part = grids[colour]
        for turn in range(2):
            part = part[0] + view_swap(part[1], colour, turn)
        part = part.reshape(-1, LANES)
        rows = part.shape[0]
        if colour == LAST:
            part = jnp.concatenate([part, packed], axis=0)
        for turn in (2, 3):
            part = part + view_swap(part, colour, turn)
        got = view_swap(part, colour, 1)
        sent = jnp.concatenate([part[:rows], got[:rows]], axis=0)
        if colour == LAST:
            packed = part[rows:] + got[rows:]
            sent = jnp.concatenate([sent, packed], axis=0)
        sources += [part, got, view_swap(sent, colour, 0)]

    channels = latent_grid.shape[1]
    grid, one_t, two, three, four = run_finish(info, sources, packed, channels, voxels)
    return (image, grid, one_t.T, two, three, four)


def solution(mesh):
    in_specs = (
        P("brick", None, None),
        P(),
        P(),
        P(),
        P(),
        P("view"),
        P("view", "brick", None, None),
        P("view", None, "brick"),
    )
    out_specs = (P("view", None, "brick"), P("brick", None, None), P(), P(), P(), P())
    return jax.shard_map(work, mesh=mesh, in_specs=in_specs, out_specs=out_specs, check_vma=False)
```

```python
import functools

import jax
import jax.numpy as jnp
from jax import lax
from jax.experimental import pallas as pl
from jax.experimental.pallas import tpu as pltpu
from jax.sharding import PartitionSpec as P


F32 = jnp.float32
BF16 = jnp.bfloat16
NT = (((1,), (1,)), ((), ()))
STEPS = 8
TILE = 512
LANES = 128
PARTS = TILE // LANES
OUT_ROWS = 40
SIZES = (3, 3, 2)
FIRSTS = tuple(sum(SIZES[:c]) for c in range(len(SIZES)))
COLOURS = len(SIZES)
LAST = COLOURS - 1
HALVED = (1, 2)
SPLIT = 3


def mm(a, b):
    return jnp.dot(a, b, preferred_element_type=F32)


def mm_nt(a, b):
    return lax.dot_general(a, b, NT, preferred_element_type=F32)


def place_to_tile(place, brick):
    return jnp.bitwise_xor(jnp.bitwise_xor(place, jnp.right_shift(place, 2) * 2), brick)


def one_hot(local):
    low = jnp.bitwise_and(local, LANES - 1)
    rows = lax.broadcasted_iota(jnp.int16, (LANES, local.shape[1]), 0)
    match = rows == jnp.broadcast_to(low.astype(jnp.int16), rows.shape)
    return jnp.where(match, jnp.ones(rows.shape, BF16), jnp.zeros(rows.shape, BF16))


def row_of(array, step):
    return array[step : step + 1, :]


def colour_at(colour_ref, step):
    return colour_ref[0, :, step * TILE : (step + 1) * TILE].astype(F32)


def forward_kernel(
    first, brick_ref, grid_ref, samples_ref, one_ref, two_ref, three_ref, four_ref,
    partial_ref, trans_ref, hidden_ref, feature_ref, colour_ref, ray_ref, last_ref,
):
    tile = place_to_tile(pl.program_id(0) + first, brick_ref[0])
    spacing = 2.0 / (STEPS * 8)
    channels = grid_ref.shape[0]
    row = pl.program_id(0)
    for step in range(STEPS):
        span = pl.ds(step * TILE, TILE)
        local = jnp.bitwise_and(samples_ref[step : step + 1, :], TILE - 1)
        base = step * (grid_ref.shape[1] // STEPS) + tile * TILE
        pieces = [
            grid_ref[:, pl.ds(pl.multiple_of(base + k * LANES, LANES), LANES)]
            for k in range(PARTS)
        ]
        wide = mm(jnp.concatenate(pieces, axis=0), one_hot(local))
        high = jnp.broadcast_to(jnp.right_shift(local, 7), (channels, TILE))
        picked = wide[:channels]
        for k in range(1, PARTS):
            picked = jnp.where(high == k, wide[k * channels : (k + 1) * channels], picked)
        feature_ref[0, :, span] = picked.astype(BF16)
    for layer, weight_ref in enumerate((one_ref, two_ref, three_ref)):
        for step in range(STEPS):
            span = pl.ds(step * TILE, TILE)
            value = feature_ref[0, :, span] if layer == 0 else hidden_ref[0, layer - 1, :, span]
            half = mm(weight_ref[...], value)
            gate = 1.0 + jnp.tanh(half)
            hidden = half * gate
            hidden = hidden.astype(BF16)
            gate = gate.astype(BF16)
            hidden_ref[0, layer, :, span] = hidden
            hidden_ref[0, 3 + layer, :, span] = gate + hidden * (2.0 - gate)
    for step in range(STEPS):
        span = pl.ds(step * TILE, TILE)
        output = mm(four_ref[...], hidden_ref[0, 2, :, span])
        colour_ref[0, :, span] = (0.5 + 0.5 * jnp.tanh(output[:32])).astype(BF16)
        last_ref[step : step + 1, :] = output[32:33]
    half = last_ref[...]
    raw = half + half
    depth = (jnp.maximum(raw, 0.0) + jnp.log1p(jnp.exp(-jnp.abs(raw)))) * spacing
    running = [row_of(depth, 0)]
    for step in range(1, STEPS):
        running.append(running[-1] + row_of(depth, step))
    earlier = jnp.concatenate([jnp.zeros_like(running[0])] + running[:-1], axis=0)
    running = jnp.concatenate(running, axis=0)
    through = jnp.exp(-running)
    small = depth * (1.0 - depth * (0.5 - depth * (1.0 / 6.0 - depth * (1.0 / 24.0))))
    absorbed = jnp.where(depth < 0.02, small, 1.0 - jnp.exp(-depth))
    factor = jnp.exp(-earlier) * absorbed
    ray_ref[0, 0] = factor
    ray_ref[0, 1] = through
    ray_ref[0, 2] = spacing * (0.5 + 0.5 * jnp.tanh(half))
    image = row_of(factor, 0) * colour_at(colour_ref, 0)
    for step in range(1, STEPS):
        image = image + row_of(factor, step) * colour_at(colour_ref, step)
    partial_ref[0] = image
    trans_ref[pl.ds(row, 1), :] = through[STEPS - 1 : STEPS, :]


def backward_kernel(
    colour, brick_ref, samples_ref, near_ref, far_ref, weight_ref, behind_ref, hidden_ref, feature_ref,
    colour_ref, ray_ref, one_t_ref, two_t_ref, three_t_ref, four_t_ref, before_ref,
    grid_ref, packed_ref, cot_ref, out_ref, feature_cot_ref,
):
    place = pl.program_id(0) + FIRSTS[colour]
    channels = feature_ref.shape[1]

    @pl.when(pl.program_id(0) == 0)
    def _():
        if colour == 0:
            packed_ref[...] = jnp.zeros_like(packed_ref)
        else:
            packed_ref[...] = before_ref[...]

    weight = weight_ref[pl.ds(place, 1), :]
    trans_grad = weight * behind_ref[pl.ds(place, 1), :]
    factor = ray_ref[0, 0]
    through = ray_ref[0, 1]
    scaled = weight * jnp.where(place < 4, near_ref[0], far_ref[0])
    dots = jnp.concatenate(
        [
            jnp.sum(scaled * colour_at(colour_ref, step), axis=0, keepdims=True)
            for step in range(STEPS)
        ],
        axis=0,
    )
    taken = factor * dots
    later = [row_of(through, STEPS - 1) * trans_grad]
    for step in range(STEPS - 1, 0, -1):
        later.append(later[-1] + row_of(taken, step))
    depth_grad = through * dots - jnp.concatenate(later[::-1], axis=0)
    last = depth_grad * ray_ref[0, 2]
    first_row = lax.broadcasted_iota(jnp.int32, (OUT_ROWS - 32, TILE), 0) == 0
    for step in range(STEPS):
        span = pl.ds(step * TILE, TILE)
        shade = colour_at(colour_ref, step)
        out_ref[:, span] = jnp.concatenate(
            [
                (shade - shade * shade) * (row_of(factor, step) * scaled),
                jnp.where(first_row, row_of(last, step), 0.0),
            ],
            axis=0,
        ).astype(BF16)
    sums = [0.0] * 4
    for layer in (2, 1, 0):
        for step in range(STEPS):
            span = pl.ds(step * TILE, TILE)
            weight_t = (two_t_ref, three_t_ref, four_t_ref)[layer][...]
            cot = out_ref[:, span] if layer == 2 else cot_ref[layer + 1, :, span]
            cot_ref[layer, :, span] = (
                mm(weight_t, cot).astype(BF16) * hidden_ref[0, 3 + layer, :, span]
            )
            if step % 2 == 1:
                pair = pl.ds((step - 1) * TILE, 2 * TILE)
                cot = out_ref[:, pair] if layer == 2 else cot_ref[layer + 1, :, pair]
                sums[layer + 1] += mm_nt(cot, hidden_ref[0, layer, :, pair])
    for step in range(STEPS):
        span = pl.ds(step * TILE, TILE)
        feature_cot_ref[:, span] = mm(one_t_ref[...], cot_ref[0, :, span]).astype(BF16)
        if step % 2 == 1:
            pair = pl.ds((step - 1) * TILE, 2 * TILE)
            sums[0] += mm_nt(feature_ref[0, :, pair], cot_ref[0, :, pair])
    for step in range(STEPS):
        feature_cot = feature_cot_ref[:, pl.ds(step * TILE, TILE)].astype(F32)
        local = jnp.bitwise_and(samples_ref[step : step + 1, :], TILE - 1)
        high = jnp.broadcast_to(jnp.right_shift(local, 7), (channels, TILE))
        spread = jnp.concatenate(
            [jnp.where(high == k, feature_cot, 0.0) for k in range(PARTS)], axis=0
        ).astype(BF16)
        half = jnp.bitwise_xor(step // 4, brick_ref[2 + colour])
        quarter = jnp.bitwise_xor(step // 2 % 2, brick_ref[2 + COLOURS + colour])
        grid_ref[half, quarter, 0, step % 2] = mm_nt(spread, one_hot(local))

    for half in range(2):
        rows = slice(32 * half, 32 * half + 32)
        packed_ref[0, :, 128 * half : 128 * half + 64] += 0.5 * sums[1][rows]
        packed_ref[0, :, 128 * half + 64 : 128 * half + 128] += 0.5 * sums[2][rows]
    packed_ref[0, :, 256:320] += sums[3][0:32]
    packed_ref[0, 0:8, 384:448] += sums[3][32:40]
    packed_ref[0, 0:16, 320:384] += 0.5 * sums[0]


def prepare_kernel(
    grid_in_ref, samples_in_ref, given_in_ref, one_t_in_ref, two_in_ref, three_in_ref, four_in_ref,
    grid_ref, samples_ref, given_ref, one_ref, two_ref, three_ref, four_ref,
    one_t_ref, two_t_ref, three_t_ref, four_t_ref,
):
    grid_ref[...] = grid_in_ref[...]
    samples_ref[...] = samples_in_ref[...]
    given_ref[...] = given_in_ref[...]
    one_t = one_t_in_ref[...].astype(F32) * 0.5
    one_ref[...] = one_t.T.astype(BF16)
    one_t_ref[...] = one_t.astype(BF16)
    for in_ref, plain_ref, turned_ref in (
        (two_in_ref, two_ref, two_t_ref),
        (three_in_ref, three_ref, three_t_ref),
    ):
        layer = in_ref[...].astype(F32) * 0.5
        plain_ref[...] = layer.astype(BF16)
        turned_ref[...] = layer.T.astype(BF16)
    four = four_in_ref[...].astype(F32)
    four = jnp.concatenate([four, jnp.zeros((OUT_ROWS - four.shape[0], 64), F32)], axis=0)
    four_ref[...] = (four * 0.5).astype(BF16)
    four_t_ref[...] = four.T.astype(BF16)


def flip_rows(array, flip):
    if flip == 4:
        return pltpu.roll(array, 4, 0)
    rows = lax.broadcasted_iota(jnp.int32, array.shape, 0)
    upper = jnp.bitwise_and(rows, flip) == 0
    return jnp.where(upper, pltpu.roll(array, 8 - flip, 0), pltpu.roll(array, flip, 0))


def dots_kernel(near_ref, far_ref, part_low_ref, part_high_ref, trans_low_ref, trans_high_ref, out_ref):
    out_ref[0, 0:SPLIT, :] = trans_low_ref[...]
    out_ref[0, SPLIT:8, :] = trans_high_ref[...]
    for p in range(8):
        given = near_ref[p] if p < 4 else far_ref[p - 4]
        part = part_low_ref[p] if p < SPLIT else part_high_ref[p - SPLIT]
        out_ref[1, p : p + 1, :] = jnp.sum(given * part, axis=0, keepdims=True)


def first_of(rank, level, shape):
    bit = jnp.bitwise_and(jnp.right_shift(rank, level), 1)
    return jnp.full(shape, bit, jnp.int32) == 0


def joined(first, total, dots, other_total, other_dots):
    return total * other_total, jnp.where(
        first, dots + total * other_dots, other_dots + other_total * dots
    )


def quad_kernel(info_ref, order_ref, own_ref, one_ref, two_ref, three_ref, out_ref, next_ref):
    total, dots = own_ref[0], own_ref[1]
    rank = jnp.bitwise_xor(info_ref[0], order_ref[0])
    ones, zeros = jnp.ones_like(total), jnp.zeros_like(total)
    first = first_of(rank, 0, total.shape)
    one_total, one_dots = (flip_rows(one_ref[i], 1) for i in range(2))
    two_total, two_dots = (flip_rows(two_ref[i], 2) for i in range(2))
    three_total, three_dots = (flip_rows(flip_rows(three_ref[i], 1), 2) for i in range(2))
    behind = jnp.where(first, one_dots, zeros)
    after = jnp.where(first, one_total, ones)
    front = jnp.where(first, ones, one_total)
    total, dots = joined(first, total, dots, one_total, one_dots)
    other_total, other_dots = joined(first, two_total, two_dots, three_total, three_dots)
    first = first_of(rank, 1, total.shape)
    next_ref[0] = jnp.where(first, front, front * other_total)
    next_ref[1] = jnp.where(first, behind + after * other_dots, behind)
    next_ref[2] = jnp.where(first, after * other_total, after)
    out_ref[0], out_ref[1] = joined(first, total, dots, other_total, other_dots)


def eight_kernel(
    info_ref, order_ref, got_ref, state_ref, part_low_ref, part_high_ref,
    front_ref, behind_ref, image_near_ref, image_far_ref,
):
    got_total, got_dots = flip_rows(got_ref[0], 4), flip_rows(got_ref[1], 4)
    rank = jnp.bitwise_xor(info_ref[0], order_ref[0])
    first = first_of(rank, 2, got_total.shape)
    front = jnp.where(first, state_ref[0], state_ref[0] * got_total)
    front_ref[...] = front
    behind_ref[...] = jnp.where(first, state_ref[1] + state_ref[2] * got_dots, state_ref[1])
    for p in range(8):
        part = part_low_ref[p] if p < SPLIT else part_high_ref[p - SPLIT]
        image_ref = image_near_ref if p < 4 else image_far_ref
        image_ref[p % 4] = front[p : p + 1] * part


def finish_kernel(info_ref, *refs):
    sources, (packed_in_ref, grid_ref, one_t_ref, two_ref, three_ref, four_ref) = refs[: 4 * COLOURS], refs[4 * COLOURS :]
    channels = grid_ref.shape[1]
    slab = grid_ref.shape[2] // STEPS

    unit = PARTS * channels
    for colour in range(COLOURS):
        rows = 2 * SIZES[colour] * unit
        for part in range(4):
            source = sources[4 * colour + part]
            skip = rows if part == 3 and colour not in HALVED else 0
            half = jnp.bitwise_xor(info_ref[2 + colour], part // 2)
            quarter = jnp.bitwise_xor(info_ref[2 + COLOURS + colour], part % 2)
            for at in range(SIZES[colour]):
                tile = place_to_tile(FIRSTS[colour] + at, info_ref[0])
                for step in range(2):
                    start = (half * 4 + quarter * 2 + step) * slab + tile * TILE
                    for k in range(PARTS):
                        row = skip + (at * 2 + step) * unit + k * channels
                        span = pl.ds(pl.multiple_of(start + k * LANES, LANES), LANES)
                        grid_ref[0, :, span] = source[row : row + channels, :]
    packed_in_ref = packed_in_ref[...] + sources[4 * LAST + 3][-104:, :]
    one_t_ref[...] = packed_in_ref[64:80, 64:128]
    two_ref[...] = packed_in_ref[0:64, 0:64]
    three_ref[...] = packed_in_ref[0:64, 64:128]
    four_ref[...] = packed_in_ref[64:97, 0:64]


VMEM = pl.BlockSpec(memory_space=pltpu.VMEM)
SMEM = pl.BlockSpec(memory_space=pltpu.SMEM)
SMALL = pltpu.CompilerParams(vmem_limit_bytes=4 * 2**20)


def run_prepare(grid, samples, given, one_t, two, three, four):
    channels = one_t.shape[0]
    shapes = [(64, channels), (64, 64), (64, 64), (OUT_ROWS, 64)]
    shapes += [shape[::-1] for shape in shapes]
    return pl.pallas_call(
        prepare_kernel,
        out_shape=[
            jax.ShapeDtypeStruct(grid.shape, grid.dtype),
            jax.ShapeDtypeStruct(samples.shape, samples.dtype),
            jax.ShapeDtypeStruct(given.shape, given.dtype),
            *[jax.ShapeDtypeStruct(shape, BF16) for shape in shapes],
        ],
        in_specs=[VMEM] * 7,
        out_specs=[VMEM] * 11,
        compiler_params=SMALL,
        name="prepare",
    )(grid, samples, given, one_t, two, three, four)


def run_dots(*arrays):
    return pl.pallas_call(
        dots_kernel,
        out_shape=jax.ShapeDtypeStruct((2, 8, TILE), F32),
        in_specs=[VMEM] * 6,
        out_specs=VMEM,
        compiler_params=SMALL,
        name="dots",
    )(*arrays)


def run_quad(info, order, *arrays):
    return pl.pallas_call(
        quad_kernel,
        out_shape=[jax.ShapeDtypeStruct((n, 8, TILE), F32) for n in (2, 3)],
        in_specs=[SMEM, SMEM] + [VMEM] * 4,
        out_specs=[VMEM] * 2,
        compiler_params=SMALL,
        name="quad",
    )(info, order, *arrays)


def run_eight(info, order, *arrays):
    shapes = [(8, TILE), (8, TILE), (4, 32, TILE), (4, 32, TILE)]
    return pl.pallas_call(
        eight_kernel,
        out_shape=[jax.ShapeDtypeStruct(shape, F32) for shape in shapes],
        in_specs=[SMEM, SMEM] + [VMEM] * 4,
        out_specs=[VMEM] * 4,
        compiler_params=SMALL,
        name="eight",
    )(info, order, *arrays)


def whole(shape):
    return pl.BlockSpec(shape, lambda p, brick: (0,) * len(shape))


def at_place(shape):
    return pl.BlockSpec((1,) + shape, lambda p, brick: (p,) + (0,) * len(shape))


def run_forward(first, count, brick, grid, samples, one, two, three, four):
    wide = STEPS * TILE
    channels = grid.shape[0]
    shapes = [
        jax.ShapeDtypeStruct((count, 32, TILE), F32),
        jax.ShapeDtypeStruct((count, TILE), F32),
        jax.ShapeDtypeStruct((count, 6, 64, wide), BF16),
        jax.ShapeDtypeStruct((count, channels, wide), BF16),
        jax.ShapeDtypeStruct((count, 32, wide), BF16),
        jax.ShapeDtypeStruct((count, 3, STEPS, TILE), F32),
    ]
    return pl.pallas_call(
        functools.partial(forward_kernel, first),
        out_shape=shapes,
        grid_spec=pltpu.PrefetchScalarGridSpec(
            num_scalar_prefetch=1,
            grid=(count,),
            in_specs=[
                whole(grid.shape),
                pl.BlockSpec(
                    (STEPS, TILE), lambda p, brick: (0, place_to_tile(p + first, brick[0]))
                ),
                whole(one.shape),
                whole(two.shape),
                whole(three.shape),
                whole(four.shape),
            ],
            out_specs=[
                at_place((32, TILE)),
                whole((count, TILE)),
                at_place((6, 64, wide)),
                at_place((channels, wide)),
                at_place((32, wide)),
                at_place((3, STEPS, TILE)),
            ],
            scratch_shapes=[pltpu.VMEM((STEPS, TILE), F32)],
        ),
        cost_estimate=pl.CostEstimate(
            flops=250_000_000 * count,
            bytes_accessed=4_000_000 * count,
            transcendentals=1_000_000 * count,
        ),
        compiler_params=pltpu.CompilerParams(vmem_limit_bytes=14 * 2**20),
        name="forward",
    )(brick, grid, samples, one, two, three, four)


def run_backward(colour, brick, samples, near, far, weight, behind, saved, layers, before):
    count = SIZES[colour]
    first = FIRSTS[colour]
    skip = first if first < SPLIT else first - SPLIT
    wide = STEPS * TILE
    hidden, feature, shade, ray = saved
    channels = feature.shape[1]

    def later(shape):
        return pl.BlockSpec((1,) + shape, lambda p, brick: (p + skip,) + (0,) * len(shape))

    return pl.pallas_call(
        functools.partial(backward_kernel, colour),
        out_shape=[
            jax.ShapeDtypeStruct((2, 2, count, 2, PARTS * channels, LANES), F32),
            jax.ShapeDtypeStruct((1, 32, TILE), F32),
        ],
        grid_spec=pltpu.PrefetchScalarGridSpec(
            num_scalar_prefetch=1,
            grid=(count,),
            in_specs=[
                pl.BlockSpec(
                    (STEPS, TILE), lambda p, brick: (0, place_to_tile(p + first, brick[0]))
                ),
                pl.BlockSpec((1, 32, TILE), lambda p, brick: (jnp.minimum(p + first, 3), 0, 0)),
                pl.BlockSpec((1, 32, TILE), lambda p, brick: (jnp.maximum(p + first, 4) - 4, 0, 0)),
                whole(weight.shape),
                whole(behind.shape),
                later((6, 64, wide)),
                later((channels, wide)),
                later((32, wide)),
                later((3, STEPS, TILE)),
                *[whole(layer.shape) for layer in layers],
                whole((1, 32, TILE)),
            ],
            out_specs=[
                pl.BlockSpec(
                    (2, 2, 1, 2, PARTS * channels, LANES), lambda p, brick: (0, 0, p, 0, 0, 0)
                ),
                whole((1, 32, TILE)),
            ],
            scratch_shapes=[
                pltpu.VMEM((3, 64, wide), BF16),
                pltpu.VMEM((OUT_ROWS, wide), BF16),
                pltpu.VMEM((channels, wide), BF16),
            ],
        ),
        cost_estimate=pl.CostEstimate(
            flops=500_000_000 * count, bytes_accessed=4_500_000 * count, transcendentals=0
        ),
        compiler_params=pltpu.CompilerParams(vmem_limit_bytes=14 * 2**20),
        name="backward",
    )(
        brick, samples, near, far, weight, behind, hidden, feature, shade, ray, *layers, before
    )


def run_finish(info, sources, packed, channels, voxels):
    return pl.pallas_call(
        finish_kernel,
        out_shape=[
            jax.ShapeDtypeStruct((1, channels, voxels), F32),
            jax.ShapeDtypeStruct((channels, 64), F32),
            jax.ShapeDtypeStruct((64, 64), F32),
            jax.ShapeDtypeStruct((64, 64), F32),
            jax.ShapeDtypeStruct((33, 64), F32),
        ],
        in_specs=[SMEM] + [VMEM] * (4 * COLOURS + 1),
        out_specs=[VMEM] * 5,
        compiler_params=pltpu.CompilerParams(vmem_limit_bytes=14 * 2**20),
        name="finish",
    )(info, *sources, packed)


def swap_brick(array, flip):
    return lax.ppermute(array, "brick", [(i, i ^ flip) for i in range(8)])


def link_of(colour, turn, odd):
    return (2 * colour + turn + 2 * odd) % 4


def view_swap(array, colour, turn):
    pairs = []
    for view in range(16):
        y, x = view // 4, view % 4
        for brick in range(8):
            dim = link_of(colour, turn, brick % 2)
            flip = 1 if dim < 2 else 3
            other = y * 4 + (x ^ flip) if dim % 2 == 0 else (y ^ flip) * 4 + x
            pairs.append((brick * 16 + view, brick * 16 + other))
    return lax.ppermute(array, ("brick", "view"), pairs)


def make_info(brick):
    view = lax.axis_index("view")
    y = jnp.right_shift(view, 2)
    x = jnp.bitwise_and(view, 3)
    bits = [
        jnp.bitwise_and(x ^ (x >> 1), 1),
        jnp.bitwise_and(y ^ (y >> 1), 1),
        x >> 1,
        y >> 1,
    ]
    odd = jnp.bitwise_and(brick, 1) == 1
    values = [brick, brick]
    for turn in range(2):
        for colour in range(COLOURS):
            even_bit, odd_bit = (bits[link_of(colour, turn, at)] for at in range(2))
            values.append(jnp.where(odd, odd_bit, even_bit))
    return jnp.stack(values).astype(jnp.int32)


def work(
    latent_grid, layer_one, layer_two, layer_three, layer_four, view_order, samples, pixel_grad
):
    brick = lax.axis_index("brick")
    info = make_info(brick)
    voxels = latent_grid.shape[2]

    latent, index, given, *layers = run_prepare(
        *[
            pltpu.with_memory_space_constraint(array, pltpu.HBM)
            for array in (
                latent_grid[0], samples[0, 0], pixel_grad, layer_one.T, layer_two, layer_three, layer_four,
            )
        ]
    )
    plain, turned = layers[:4], layers[4:]

    near = [given] + [swap_brick(pixel_grad, flip) for flip in (1, 2, 3)]
    part_low, trans_low, *saved_low = run_forward(0, SPLIT, info, latent, index, *plain)
    near = jnp.concatenate(near, axis=0)
    far = swap_brick(near, 6)
    part_high, trans_high, *saved_high = run_forward(SPLIT, 8 - SPLIT, info, latent, index, *plain)

    own = run_dots(near, far, part_low, part_high, trans_low, trans_high)
    got = [swap_brick(own, flip) for flip in (2, 3, 1)]
    own, state = run_quad(info, view_order, own, got[2], got[0], got[1])
    front, behind, image_near, image_far = run_eight(
        info, view_order, swap_brick(own, 6), state, part_low, part_high
    )

    image = image_near + swap_brick(image_far, 6)
    got = [swap_brick(image[k : k + 1], k) for k in (1, 2, 3)]
    image = image[:1] + got[0] + (got[1] + got[2])

    packed = jnp.zeros((1, 32, TILE), F32)
    grids = []
    for colour in range(COLOURS):
        saved = saved_low if FIRSTS[colour] < SPLIT else saved_high
        grid, packed = run_backward(
            colour, info, index, near, far, front, behind, saved, turned, packed
        )
        grids.append(grid)
    got = [swap_brick(packed, flip) for flip in (1, 2, 3)]
    packed = packed + got[0] + (got[1] + got[2])
    packed = packed + swap_brick(packed, 6)
    packed = jnp.concatenate([packed[0, :, k * LANES : (k + 1) * LANES] for k in range(4)], axis=0)
    packed = packed[:104]

    sources = []
    for colour in range(COLOURS):
        part = grids[colour]
        for turn in range(2):
            part = part[0] + view_swap(part[1], colour, turn)
        part = part.reshape(-1, LANES)
        rows = part.shape[0]
        if colour == LAST:
            part = jnp.concatenate([part, packed], axis=0)
        for turn in (2, 3):
            part = part + view_swap(part, colour, turn)
        got = view_swap(part, colour, 1)
        halved = colour in HALVED
        sent = got[:rows] if halved else jnp.concatenate([part[:rows], got[:rows]], axis=0)
        if colour == LAST:
            packed = part[rows:] + got[rows:]
            sent = jnp.concatenate([sent, packed], axis=0)
        far = view_swap(sent, colour, 0)
        first = view_swap(part[:rows], colour, 0) if halved else far
        sources += [part, got, first, far]

    channels = latent_grid.shape[1]
    grid, one_t, two, three, four = run_finish(info, sources, packed, channels, voxels)
    return (image, grid, one_t.T, two, three, four)


def solution(mesh):
    in_specs = (
        P("brick", None, None),
        P(),
        P(),
        P(),
        P(),
        P("view"),
        P("view", "brick", None, None),
        P("view", None, "brick"),
    )
    out_specs = (P("view", None, "brick"), P("brick", None, None), P(), P(), P(), P())
    return jax.shard_map(work, mesh=mesh, in_specs=in_specs, out_specs=out_specs, check_vma=False)
```
